32 devices in a mesh: depth: 4 (over y, core), tile: 8 (over z, x).
Axes of the slice: x: 2, y: 2, z: 4, core: 2. Of those that a mesh axis runs over, the one named last changes fastest.
Arguments:
- density: int32 [128, 512, 1024], P('depth', 'tile'), may hold values from 0 to 255
- view_flip: int32 [8], P('tile'), may hold values from 0 to 1
- tf_coeff: float32 [4, 4], replicated, may hold values from -4 to 4
Outputs:
- shaded: float32 [3, 512, 1024], P(None, 'tile', 'depth')
The draws below stay inside these ranges and needn't reach their ends.
All inputs are finite; a program needn't handle non-finite values.
Results may differ from the reference program's by a relative error of at most 0.0003.
Values may be sent and summed in bfloat16 or wider, within the bound.
No kernel may reach another device: no remote copies, remote signals or barrier semaphores. Data moves between devices by JAX's collectives and lax.ppermute only.
A program may use at most 192 MiB of HBM per device.

```python
import jax
import jax.numpy as jnp
from jax import lax

ROWS_DEV = 64
W = 1024
RADIUS = 8
DEG = 4
H = 512
NZ = 128
N_TILE = 8


def octave(seed_key, period, amplitude):
    extents = ((NZ + period - 1) // period + 2, (H + period - 1) // period + 2, (W + period - 1) // period + 2)
    result = jax.random.randint(seed_key, extents, -amplitude, amplitude + 1, dtype=jnp.int32)
    for along_axis, length in ((0, NZ), (1, H), (2, W)):
        cell_index = jnp.arange(length, dtype=jnp.int32)
        lower_cell = cell_index // period
        fraction = cell_index % period
        view_shape = [1, 1, 1]
        view_shape[along_axis] = length
        fraction = fraction.reshape(view_shape)
        first = jnp.take(result, lower_cell, axis=along_axis)
        second = jnp.take(result, lower_cell + 1, axis=along_axis)
        result = (first * (period - fraction) + second * fraction) // period
    return result


def sphere_distance(seed_key, z_low, z_high):
    centre_z = jax.random.randint(jax.random.fold_in(seed_key, 1), (), z_low, z_high, dtype=jnp.int32)
    centre_y = jax.random.randint(jax.random.fold_in(seed_key, 2), (), 0, H, dtype=jnp.int32)
    centre_x = jax.random.randint(jax.random.fold_in(seed_key, 3), (), 0, W, dtype=jnp.int32)
    offset_z = jnp.arange(NZ, dtype=jnp.int32) - centre_z
    offset_y = jnp.arange(H, dtype=jnp.int32) - centre_y
    offset_x = jnp.arange(W, dtype=jnp.int32) - centre_x
    return (offset_z * offset_z)[:, None, None] + (offset_y * offset_y)[None, :, None] + (offset_x * offset_x)[None, None, :]


def draw_density(key, part):
    field = jnp.int32(110) + octave(jax.random.fold_in(key, 11), 64, 90)
    field = field + octave(jax.random.fold_in(key, 12), 16, 50)
    field = field + octave(jax.random.fold_in(key, 13), 4, 25)
    field = field + jax.random.randint(jax.random.fold_in(key, 14), (NZ, H, W), -12, 13, dtype=jnp.int32)
    for blob_number in range(6):
        blob_key = jax.random.fold_in(key, 100 + blob_number)
        distance = sphere_distance(blob_key, 0, NZ)
        radius = jax.random.randint(jax.random.fold_in(blob_key, 4), (), 6, 41, dtype=jnp.int32)
        polarity = 2 * jax.random.randint(jax.random.fold_in(blob_key, 5), (), 0, 2, dtype=jnp.int32) - 1
        hollow = jax.random.randint(jax.random.fold_in(blob_key, 6), (), 0, 2, dtype=jnp.int32)
        outer = (radius + 3) * (radius + 3)
        inner = jnp.where(hollow == 1, radius * radius, jnp.int32(0))
        inside = (distance <= outer) & (distance >= inner)
        field = field + jnp.where(inside, 70 * polarity, jnp.int32(0))
    dense_key = jax.random.fold_in(key, 200)
    dense_distance = sphere_distance(dense_key, 0, NZ // 4)
    dense_radius = jax.random.randint(jax.random.fold_in(dense_key, 4), (), 6, 17, dtype=jnp.int32)
    field = jnp.where(dense_distance <= dense_radius * dense_radius, jnp.int32(255), field)
    void_key = jax.random.fold_in(key, 201)
    void_distance = sphere_distance(void_key, 3 * NZ // 4, NZ)
    void_radius = jax.random.randint(jax.random.fold_in(void_key, 4), (), 6, 17, dtype=jnp.int32)
    field = jnp.where(void_distance <= void_radius * void_radius, jnp.int32(0), field)
    return jnp.clip(field, 0, 255).astype(jnp.int32)


def touch_ends(drawn, key, least, high):
    dims = drawn.shape
    spot = [jax.random.randint(jax.random.fold_in(key, axis), (), 0, dims[axis]) for axis in range(len(dims))]
    drawn = drawn.at[tuple(spot)].set(least)
    longest = dims.index(max(dims))
    spot[longest] = (spot[longest] + 1) % dims[longest]
    return drawn.at[tuple(spot)].set(high)


def normal_values(own_key, shape, scale, reach, kind=jnp.bfloat16):
    return jnp.clip(scale * jax.random.normal(own_key, shape, jnp.float32), -reach, reach).astype(kind)


def setup_inputs(seed: int = 0) -> dict:
    keys = jax.random.split(jax.random.key(seed), 4)
    density = draw_density(jax.random.fold_in(keys[3], 71), 0)
    view_flip = touch_ends(jax.random.randint(keys[1], (N_TILE,), 0, 2), jax.random.fold_in(keys[1], 1), 0, 1).astype(jnp.int32)
    tf_coeff = normal_values(keys[2], (4, DEG), 1.0, 4.0, jnp.float32)
    return {"density": density, "view_flip": view_flip, "tf_coeff": tf_coeff}


opacity_scale = 0.008
grad_half = 1.0
light_x = 0.48
light_y = 0.6
light_z = 0.64
spatial_scale = 1.0 / 72.0
depth_weight = 20.0
normal_weight = 2.0

def polynomial(coeff, scaled):
    return coeff[0] + scaled * (coeff[1] + scaled * (coeff[2] + scaled * coeff[3]))

def integrate(field, flipped, tf_coeff, depth_start, depth_total):
    centre = field[1:-1, 1:-1, :]
    sideways = jnp.pad(centre, ((0, 0), (0, 0), (1, 1)))
    grad_x = (sideways[:, :, 2:] - sideways[:, :, :-2]) * grad_half
    grad_y = (field[1:-1, 2:, :] - field[1:-1, :-2, :]) * grad_half
    grad_z = (field[2:, 1:-1, :] - field[:-2, 1:-1, :]) * grad_half
    scaling = lax.rsqrt(1.0 + grad_x * grad_x + grad_y * grad_y + grad_z * grad_z)
    normal_x = grad_x * scaling
    normal_y = grad_y * scaling
    normal_z = grad_z * scaling
    shading = 0.35 + 0.65 * jnp.abs(light_x * normal_x + light_y * normal_y + light_z * normal_z)
    scaled = 2.0 * centre - 1.0
    sigma = opacity_scale * jax.nn.softplus(polynomial(tf_coeff[0], scaled))
    running = jnp.cumsum(sigma, axis=0)
    total = running[-1]
    optical = jnp.where(flipped == 1, total - running, running - sigma)
    weight = jnp.exp(-optical) * (1.0 - jnp.exp(-sigma))
    cells = sigma.shape[0]
    height = ((depth_start + jnp.arange(cells, dtype=jnp.int32)).astype(jnp.float32) + 0.5) / depth_total
    height = jnp.where(flipped == 1, 1.0 - height, height)[:, None, None]
    planes = []
    for channel in range(1, 4):
        colour = jax.nn.sigmoid(polynomial(tf_coeff[channel], scaled)) * shading
        planes.append(lax.optimization_barrier(jnp.sum(weight * colour, axis=0)))
    planes.append(1.0 - jnp.exp(-total))
    planes.append(lax.optimization_barrier(jnp.sum(weight * height, axis=0)))
    planes.append(lax.optimization_barrier(jnp.sum(weight * normal_x, axis=0)))
    planes.append(lax.optimization_barrier(jnp.sum(weight * normal_y, axis=0)))
    planes.append(lax.optimization_barrier(jnp.sum(weight * normal_z, axis=0)))
    return jnp.stack(planes, axis=0)

def shade_image(extended, rows, cols):
    colour = extended[0:3]
    normal = extended[5:8]
    facing = jnp.maximum(light_x * normal[0] + light_y * normal[1] + light_z * normal[2], 0.0)
    lit = colour * (0.4 + 0.6 * facing)
    stacked = jnp.concatenate([extended, lit], axis=0)
    centre = extended[:, RADIUS:RADIUS + rows, RADIUS:RADIUS + cols]
    span = 2 * RADIUS + 1

    def row_step(offset_y, sums):
        numer, denom = sums
        offset_y = offset_y.astype(jnp.int32)
        rise = (offset_y - RADIUS).astype(jnp.float32)
        for offset_x in range(span):
            near = lax.dynamic_slice(stacked, (jnp.int32(0), offset_y, jnp.int32(offset_x)), (11, rows, cols))
            run = float(offset_x - RADIUS)
            exponent = -(rise * rise + run * run) * spatial_scale
            exponent = exponent - depth_weight * (centre[4] - near[4]) ** 2
            exponent = exponent - normal_weight * lax.optimization_barrier(jnp.sum((centre[5:8] - near[5:8]) ** 2, axis=0))
            weight = near[3] * jnp.exp(exponent)
            numer = numer + weight * near[8:11]
            denom = denom + weight
        return (numer, denom)
    start = (jnp.zeros((3, rows, cols), jnp.float32), jnp.zeros((rows, cols), jnp.float32))
    numer, denom = lax.fori_loop(0, span, row_step, start)
    return numer / (1.0 + denom)

def reference(density, view_flip, tf_coeff):
    padded = jnp.pad(density, ((1, 1), (1, 1), (0, 0)))

    def strip(index):
        field = lax.dynamic_slice(padded, (jnp.int32(0), index * ROWS_DEV, jnp.int32(0)), (NZ + 2, ROWS_DEV + 2, W))
        field = field.astype(jnp.float32) / 255.0
        return integrate(field, view_flip[index], tf_coeff, jnp.int32(0), NZ)
    planes = lax.map(strip, jnp.arange(N_TILE, dtype=jnp.int32))
    composited = jnp.transpose(planes, (1, 0, 2, 3)).reshape(8, H, W)
    extended = jnp.pad(composited, ((0, 0), (RADIUS, RADIUS), (RADIUS, RADIUS)))
    return shade_image(extended, H, W)
```

```python
import functools
import math

import jax
import jax.numpy as jnp
from jax import lax
from jax.experimental import pallas as pl
from jax.experimental.pallas import tpu as pltpu
from jax.sharding import PartitionSpec as P

RADIUS = 8
LANES = 128
SUB = 8
LOG2E = math.log2(math.e)
OPACITY = 0.008
LIGHT = (0.48, 0.6, 0.64)
SPATIAL = 1.0 / 72.0
DEPTH_W = 20.0
NORMAL_W = 2.0
CENTRE = 127.5


def shifts(axis):
    count = lax.axis_size(axis)
    up = [(i, i + 1) for i in range(count - 1)]
    return up, [(j, i) for i, j in up]


def swapped(block, axis, stride):
    count = lax.axis_size(axis)
    route = []
    for low in range(count):
        high = low | 1 << stride
        if high != low and high < count:
            route += [(low, high), (high, low)]
    return lax.ppermute(block, axis, route)


def integrate_kernel(
    depth_total, flip_ref, base_ref, coeff_ref, density_ref, zlo_ref, zhi_ref, ylo_ref, yhi_ref,
    out_ref, stage, field, ylo_f, yhi_f, sems,
):
    cells, rows, width = density_ref.shape
    tiles = width // LANES
    copies = []
    for z in range(cells):
        copies.append(pltpu.make_async_copy(density_ref.at[z], stage.at[z], sems.at[z]))
        copies[-1].start()
    flip = flip_ref[0]
    outside = jnp.full((SUB, LANES), -CENTRE, jnp.float32)
    for j in range(tiles):
        cols = pl.ds(j * LANES, LANES)
        ylo_f[j] = ylo_ref[:, cols].astype(jnp.float32) - CENTRE
        yhi_f[j] = yhi_ref[:, cols].astype(jnp.float32) - CENTRE
        field[0, j + 1, SUB : SUB + rows, :] = zlo_ref[:, cols].astype(jnp.float32) - CENTRE
        field[cells + 1, j + 1, SUB : SUB + rows, :] = zhi_ref[:, cols].astype(jnp.float32) - CENTRE

    def fill(z, carry):
        pltpu.make_async_copy(density_ref.at[z], stage.at[z], sems.at[z]).wait()
        for i in range(rows // SUB):
            field[z + 1, 0, pl.ds(SUB + SUB * i, SUB), :] = outside
            field[z + 1, tiles + 1, pl.ds(SUB + SUB * i, SUB), :] = outside
        for j in range(tiles):
            cols = pl.ds(j * LANES, LANES)
            field[z + 1, j + 1, SUB : SUB + rows, :] = stage[z, :, cols].astype(jnp.float32) - CENTRE
            field[z + 1, j + 1, SUB - 1 : SUB, :] = ylo_f[j, pl.ds(z, 1), :]
            field[z + 1, j + 1, SUB + rows : SUB + rows + 1, :] = yhi_f[j, pl.ds(z, 1), :]
        return carry

    lax.fori_loop(0, cells, fill, 0)

    coeffs = []
    for row in range(4):
        scale = LOG2E if row == 0 else -LOG2E
        coeffs.append([coeff_ref[row, k] * (scale / CENTRE**k) for k in range(4)])
    sign = jnp.where(flip == 1, 1.0, -1.0)
    rate = sign * OPACITY
    lx, ly, lz = (0.65 * v for v in LIGHT)
    lane = lax.broadcasted_iota(jnp.int32, (SUB, LANES), 1)
    first_lane = lane == 0
    last_lane = lane == LANES - 1
    base = base_ref[0]
    step = 1.0 / depth_total
    start = (base.astype(jnp.float32) + 0.5) * step
    finish = (base.astype(jnp.float32) + (cells - 0.5)) * step
    h_first = jnp.where(flip == 1, 1.0 - start, start)
    h_last = jnp.where(flip == 1, 1.0 - finish, finish)
    delta = jnp.where(flip == 1, -step, step)

    def poly(c, t):
        return c[0] + t * (c[1] + t * (c[2] + t * c[3]))

    def block(index, carry):
        j = index // (rows // SUB) + 1
        r = pl.multiple_of((index % (rows // SUB)) * SUB, SUB)
        at = pl.ds(r + SUB, SUB)
        zero = jnp.zeros((SUB, LANES), jnp.float32)
        tau = zero
        factor = jnp.ones((SUB, LANES), jnp.float32)
        between = zero
        sums = [zero] * 6
        below = field[0, j, at, :]
        here = field[1, j, at, :]
        for z in range(1, cells + 1):
            above = field[z + 1, j, at, :]
            left = pltpu.roll(jnp.where(last_lane, field[z, j - 1, at, :], here), 1, 1)
            right = pltpu.roll(jnp.where(first_lane, field[z, j + 1, at, :], here), LANES - 1, 1)
            gx = right - left
            gy = field[z, j, pl.ds(r + SUB + 1, SUB), :] - field[z, j, pl.ds(r + SUB - 1, SUB), :]
            gz = above - below
            norm = lax.rsqrt(gx * gx + gy * gy + (gz * gz + 255.0 * 255.0))
            shade = 0.35 + jnp.abs((lx * gx + ly * gy + lz * gz) * norm)
            tau = tau + jnp.log2(1.0 + jnp.exp2(poly(coeffs[0], here)))
            following = jnp.exp2(rate * tau)
            weight = following - factor
            factor = following
            if z < cells:
                between = between + following
            tilt = weight * norm
            lit = weight * shade
            terms = [lit * (1.0 / (1.0 + jnp.exp2(poly(coeffs[k], here)))) for k in (1, 2, 3)]
            terms += [tilt * gx, tilt * gy, tilt * gz]
            sums = [s + t for s, t in zip(sums, terms)]
            below, here = here, above
        inverse = 1.0 / factor
        flipped = flip == 1
        scale = jnp.where(flipped, inverse, -1.0)
        for k in range(3):
            out_ref[k, j - 1, pl.ds(r, SUB), :] = sums[k] * scale
            out_ref[k + 5, j - 1, pl.ds(r, SUB), :] = sums[k + 3] * scale
        out_ref[3, j - 1, pl.ds(r, SUB), :] = 1.0 - jnp.where(flipped, inverse, factor)
        out_ref[4, j - 1, pl.ds(r, SUB), :] = (h_last * factor - h_first - delta * between) * scale
        return carry

    lax.fori_loop(0, tiles * (rows // SUB), block, 0)


def integrate(density, view_flip, tf_coeff, base, depth_total, zlo, zhi, ylo, yhi):
    cells, rows, width = density.shape
    tiles = width // LANES
    smem = pl.BlockSpec(memory_space=pltpu.SMEM)
    vmem = pl.BlockSpec(memory_space=pltpu.VMEM)
    return pl.pallas_call(
        functools.partial(integrate_kernel, depth_total),
        out_shape=jax.ShapeDtypeStruct((8, tiles, rows, LANES), jnp.float32),
        in_specs=[smem, smem, smem, pl.BlockSpec(memory_space=pl.ANY), vmem, vmem, vmem, vmem],
        out_specs=vmem,
        scratch_shapes=[
            pltpu.VMEM((cells, rows, width), jnp.int32),
            pltpu.VMEM((cells + 2, tiles + 2, rows + 2 * SUB, LANES), jnp.float32),
            pltpu.VMEM((tiles, cells, LANES), jnp.float32),
            pltpu.VMEM((tiles, cells, LANES), jnp.float32),
            pltpu.SemaphoreType.DMA((cells,)),
        ],
        compiler_params=pltpu.CompilerParams(vmem_limit_bytes=48 << 20),
        name="integrate",
    )(view_flip, base, tf_coeff, density, zlo, zhi, ylo, yhi)


def shade_kernel(
    core_ref, left_ref, right_ref, top_ref, bottom_ref, out_ref, planes, feats, buf_a, buf_b, acc
):
    _, tiles, rows, _ = core_ref.shape
    blocks = rows // SUB
    halves = blocks // 4
    cols = tiles * LANES
    for k in range(8):
        for t in (0, tiles + 1):
            planes[k, t] = jnp.zeros((rows + 2 * SUB, LANES), jnp.float32)
        planes[k, 0, SUB : SUB + rows, LANES - RADIUS : LANES] = left_ref[k]
        planes[k, tiles + 1, SUB : SUB + rows, 0:RADIUS] = right_ref[k]
        for j in range(tiles):
            planes[k, j + 1, SUB : SUB + rows, :] = core_ref[k, j]
        for ref, start in ((top_ref, 0), (bottom_ref, SUB + rows)):
            planes[k, 0, start : start + SUB, LANES - RADIUS : LANES] = ref[k, :, 0:RADIUS]
            planes[k, tiles + 1, start : start + SUB, 0:RADIUS] = ref[
                k, :, cols + RADIUS : cols + 2 * RADIUS
            ]
            for j in range(tiles):
                planes[k, j + 1, start : start + SUB, :] = ref[
                    k, :, RADIUS + j * LANES : RADIUS + (j + 1) * LANES
                ]

    row_blocks = blocks + 2

    def features(index, carry):
        t = index // row_blocks
        at = pl.ds(pl.multiple_of((index % row_blocks) * SUB, SUB), SUB)
        red, green, blue, alpha, depth, nx, ny, nz = [planes[k, t, at, :] for k in range(8)]
        facing = jnp.maximum(LIGHT[0] * nx + LIGHT[1] * ny + LIGHT[2] * nz, 0.0)
        lit = 0.4 + 0.6 * facing
        own = (DEPTH_W * LOG2E) * depth * depth + (NORMAL_W * LOG2E) * (nx * nx + ny * ny + nz * nz)
        feats[0, t, at, :] = jnp.log2(jnp.maximum(alpha, 1e-37)) - own
        feats[1, t, at, :] = depth
        feats[2, t, at, :] = nx
        feats[3, t, at, :] = ny
        feats[4, t, at, :] = nz
        feats[5, t, at, :] = red * lit
        feats[6, t, at, :] = green * lit
        feats[7, t, at, :] = blue * lit
        return carry

    lax.fori_loop(0, (tiles + 2) * row_blocks, features, 0)
    lane = lax.broadcasted_iota(jnp.int32, (SUB, LANES), 1)

    def shift(index, buf, j, blk):
        offset = index - RADIUS
        run = offset.astype(jnp.float32)
        spread = -(SPATIAL * LOG2E) * run * run
        other = jnp.where(offset < 0, j, j + 2)
        border = jnp.where(offset < 0, LANES + offset, offset)
        amount = jnp.where(offset > 0, LANES - offset, -offset)
        below = lane < border
        take_other = (below & (offset >= 0)) | (jnp.logical_not(below) & (offset < 0))
        at = pl.ds(pl.multiple_of(blk * SUB, SUB), SUB)
        for k in range(8):
            mixed = jnp.where(take_other, feats[k, other, at, :], feats[k, j + 1, at, :])
            moved = pltpu.roll(mixed, amount, 1)
            if k == 0:
                moved = moved + spread
            buf[k, j, at, :] = moved

    for j in range(tiles):
        for k in range(4):
            acc[k, j] = jnp.zeros((rows, LANES), jnp.float32)

    def shift_all(index, buf):
        def one(t, carry):
            shift(index, buf, t // row_blocks, t % row_blocks)
            return carry

        lax.fori_loop(0, tiles * row_blocks, one, 0)

    share = -(-row_blocks // halves)

    def taps(buf, next_index, next_buf):
        def one(t, carry):
            j = t // halves
            half = t % halves
            first = half * 4
            if next_buf is not None:
                for b in range(share):
                    shift(next_index, next_buf, j, jnp.minimum(half * share + b, row_blocks - 1))
            own = []
            for i in range(4):
                rows_at = pl.ds(SUB + first + i, SUB, stride=blocks)
                depth = feats[1, j + 1, rows_at, :] * (2.0 * DEPTH_W * LOG2E)
                normal = [
                    feats[k, j + 1, rows_at, :] * (2.0 * NORMAL_W * LOG2E) for k in (2, 3, 4)
                ]
                own.append([depth] + normal)
            sums = [
                [acc[k, j, pl.ds(first + i, SUB, stride=blocks), :] for k in range(4)]
                for i in range(4)
            ]
            for near in range(-RADIUS, 4 + RADIUS):
                q = [
                    buf[k, j, pl.ds(SUB + first + near, SUB, stride=blocks), :] for k in range(8)
                ]
                for i in range(4):
                    dy = near - i
                    if abs(dy) > RADIUS:
                        continue
                    p = own[i]
                    power = (q[0] + p[0] * q[1]) + (p[1] * q[2] + p[2] * q[3])
                    power = power + (p[3] * q[4] - SPATIAL * LOG2E * dy * dy)
                    weight = jnp.exp2(power)
                    s = sums[i]
                    sums[i] = [
                        s[0] + weight * q[5],
                        s[1] + weight * q[6],
                        s[2] + weight * q[7],
                        s[3] + weight,
                    ]
            for i in range(4):
                for k in range(4):
                    acc[k, j, pl.ds(first + i, SUB, stride=blocks), :] = sums[i][k]
            return carry

        lax.fori_loop(0, tiles * halves, one, 0)

    shift_all(jnp.int32(0), buf_a)

    def pair(step, carry):
        taps(buf_a, 2 * step + 1, buf_b)
        taps(buf_b, 2 * step + 2, buf_a)
        return carry

    lax.fori_loop(0, RADIUS, pair, 0)
    taps(buf_a, None, None)

    for j in range(tiles):
        for b in range(blocks):
            at = pl.ds(b * SUB, SUB)
            inner = pl.ds(SUB + b * SUB, SUB)
            depth, nx, ny, nz = [feats[k, j + 1, inner, :] for k in (1, 2, 3, 4)]
            own = (DEPTH_W * LOG2E) * depth * depth + (NORMAL_W * LOG2E) * (
                nx * nx + ny * ny + nz * nz
            )
            level = jnp.exp2(-own)
            scale = level / (1.0 + level * acc[3, j, at, :])
            for k in range(3):
                out_ref[k, at, pl.ds(j * LANES, LANES)] = acc[k, j, at, :] * scale


def shade(core, left, right, top, bottom):
    _, tiles, rows, _ = core.shape
    vmem = pl.BlockSpec(memory_space=pltpu.VMEM)
    wide = (8, tiles + 2, rows + 2 * SUB, LANES)
    moved = (8, tiles, rows + 2 * SUB, LANES)
    return pl.pallas_call(
        shade_kernel,
        out_shape=jax.ShapeDtypeStruct((3, rows, tiles * LANES), jnp.float32),
        in_specs=[vmem] * 5,
        out_specs=vmem,
        scratch_shapes=[
            pltpu.VMEM(wide, jnp.float32),
            pltpu.VMEM(wide, jnp.float32),
            pltpu.VMEM(moved, jnp.float32),
            pltpu.VMEM(moved, jnp.float32),
            pltpu.VMEM((4, tiles, rows, LANES), jnp.float32),
        ],
        compiler_params=pltpu.CompilerParams(vmem_limit_bytes=32 << 20),
        name="shade",
    )(core, left, right, top, bottom)


def over_layer(front, back):
    return front + (1.0 - front[3:4]) * back


def reverse_bits(value, rounds):
    result = 0
    for level in range(rounds):
        result = result * 2 + (value >> level) % 2
    return result


def per_device(density, view_flip, tf_coeff):
    cells, rows, width = density.shape
    count = lax.axis_size("depth")
    position = lax.axis_index("depth")
    flipped = view_flip[0]
    up, down = shifts("depth")
    zlo = lax.ppermute(density[-1].astype(jnp.bfloat16), "depth", up)
    zhi = lax.ppermute(density[0].astype(jnp.bfloat16), "depth", down)
    up, down = shifts("tile")
    ylo = lax.ppermute(density[:, -1].astype(jnp.bfloat16), "tile", up)
    yhi = lax.ppermute(density[:, 0].astype(jnp.bfloat16), "tile", down)
    base = (position * cells).astype(jnp.int32).reshape(1)
    planes = integrate(density, view_flip, tf_coeff, base, cells * count, zlo, zhi, ylo, yhi)
    tiles = width // LANES
    own = tiles // count
    rounds = count.bit_length() - 1
    blocks = planes.reshape(8, count, own, rows, LANES)
    current = jnp.concatenate(
        [
            blocks[:, reverse_bits(place, rounds) : reverse_bits(place, rounds) + 1]
            for place in range(count)
        ],
        axis=1,
    )
    for level in range(rounds):
        half = current.shape[1] // 2
        upper = position // 2**level % 2
        kept = lax.dynamic_slice_in_dim(current, upper * half, half, 1)
        given = lax.dynamic_slice_in_dim(current, (1 - upper) * half, half, 1)
        partner = swapped(given, "depth", level)
        leading = upper == flipped
        front = jnp.where(leading, kept, partner)
        back = jnp.where(leading, partner, kept)
        current = over_layer(front, back)
    core = current[:, 0]
    up, down = shifts("depth")
    left = lax.ppermute(core[:, -1, :, LANES - RADIUS :], "depth", up)
    right = lax.ppermute(core[:, 0, :, :RADIUS], "depth", down)
    up, down = shifts("tile")

    def edge(start):
        pieces = [left[:, start : start + RADIUS]]
        pieces += [core[:, j, start : start + RADIUS] for j in range(own)]
        pieces += [right[:, start : start + RADIUS]]
        return jnp.concatenate(pieces, axis=2)

    top = lax.ppermute(edge(rows - RADIUS), "tile", up)
    bottom = lax.ppermute(edge(0), "tile", down)
    return shade(core, left, right, top, bottom)


def solution(mesh):
    in_specs = (P("depth", "tile", None), P("tile"), P())
    out_specs = P(None, "tile", "depth")
    return jax.shard_map(
        per_device, mesh=mesh, in_specs=in_specs, out_specs=out_specs, check_vma=False
    )
```

```python
import functools
import math

import jax
import jax.numpy as jnp
from jax import lax
from jax.experimental import pallas as pl
from jax.experimental.pallas import tpu as pltpu
from jax.sharding import PartitionSpec as P

RADIUS = 8
LANES = 128
SUB = 8
LOG2E = math.log2(math.e)
OPACITY = 0.008
LIGHT = (0.48, 0.6, 0.64)
SPATIAL = 1.0 / 72.0
DEPTH_W = 20.0
NORMAL_W = 2.0
CENTRE = 127.5


def shifts(axis):
    count = lax.axis_size(axis)
    up = [(i, i + 1) for i in range(count - 1)]
    return up, [(j, i) for i, j in up]


def swapped(block, axis, stride):
    count = lax.axis_size(axis)
    route = []
    for low in range(count):
        high = low | 1 << stride
        if high != low and high < count:
            route += [(low, high), (high, low)]
    return lax.ppermute(block, axis, route)


def edges_kernel(density_ref, zlo_ref, zhi_ref, ylo_ref, yhi_ref, planes, bands, lines, sems):
    cells, rows, width = density_ref.shape
    tiles = width // LANES
    copies = []
    for side in range(2):
        copies.append(
            pltpu.make_async_copy(
                density_ref.at[side * (cells - 1)], planes.at[side], sems.at[2 * side]
            )
        )
        copies.append(
            pltpu.make_async_copy(
                density_ref.at[:, side * (rows - SUB) : side * (rows - SUB) + SUB, :],
                bands.at[side],
                sems.at[2 * side + 1],
            )
        )
    for copy in copies:
        copy.start()
    for copy in copies:
        copy.wait()
    zlo_ref[...] = planes[0].astype(jnp.float32).astype(jnp.bfloat16)
    zhi_ref[...] = planes[1].astype(jnp.float32).astype(jnp.bfloat16)
    for side, ref in ((0, ylo_ref), (1, yhi_ref)):
        row = side * (SUB - 1)
        for z in range(cells):
            lines[z : z + 1, :] = bands[side, z, row : row + 1, :].astype(jnp.float32)
        ref[...] = lines[...].astype(jnp.bfloat16)


def edges(density):
    cells, rows, width = density.shape
    vmem = pl.BlockSpec(memory_space=pltpu.VMEM)
    plane = jax.ShapeDtypeStruct((rows, width), jnp.bfloat16)
    line = jax.ShapeDtypeStruct((cells, width), jnp.bfloat16)
    return pl.pallas_call(
        edges_kernel,
        out_shape=(plane, plane, line, line),
        in_specs=[pl.BlockSpec(memory_space=pl.ANY)],
        out_specs=[vmem] * 4,
        scratch_shapes=[
            pltpu.VMEM((2, rows, width), jnp.int32),
            pltpu.VMEM((2, cells, SUB, width), jnp.int32),
            pltpu.VMEM((cells, width), jnp.float32),
            pltpu.SemaphoreType.DMA((4,)),
        ],
        compiler_params=pltpu.CompilerParams(vmem_limit_bytes=24 << 20),
        name="edges",
    )(density)


def integrate_kernel(
    place, own, flip_ref, coeff_ref, density_ref, zlo_ref, zhi_ref, ylo_ref, yhi_ref,
    out_ref, field, zlo_f, zhi_f, sems,
):
    cells, rows, width = density_ref.shape
    tiles = width // LANES
    blocks = rows // SUB
    count = tiles // own
    position = lax.axis_index("depth")
    c, y = position % 2, position // 2 % 2
    first = (lax.rem(c + place[0], 2) + 2 * lax.rem(y + place[1], 2) + 4 * place[2]) * own
    sources = [jnp.maximum(first - 1, 0)]
    sources += [first + j for j in range(own)]
    sources += [jnp.minimum(first + own, tiles - 1)]

    def copy(b, j):
        start = pl.multiple_of(sources[j] * LANES, LANES)
        return pltpu.make_async_copy(
            density_ref.at[:, pl.ds(b * SUB, SUB), pl.ds(start, LANES)],
            field.at[:, j, pl.ds(SUB + b * SUB, SUB), :],
            sems.at[b, j],
        )

    for b in range(blocks):
        for j in range(own + 2):
            copy(b, j).start()
    flip = flip_ref[0]
    for j in range(own):
        cols = pl.ds(pl.multiple_of((first + j) * LANES, LANES), LANES)
        zlo_f[j] = zlo_ref[:, cols].astype(jnp.float32) - CENTRE
        zhi_f[j] = zhi_ref[:, cols].astype(jnp.float32) - CENTRE
        top = ylo_ref[:, cols].astype(jnp.float32).astype(jnp.int32)
        bottom = yhi_ref[:, cols].astype(jnp.float32).astype(jnp.int32)
        for z in range(cells):
            field[z, j + 1, SUB - 1 : SUB, :] = top[z : z + 1]
            field[z, j + 1, SUB + rows : SUB + rows + 1, :] = bottom[z : z + 1]

    coeffs = []
    for row in range(4):
        scale = LOG2E if row == 0 else -LOG2E
        coeffs.append([coeff_ref[row, k] * (scale / CENTRE**k) for k in range(4)])
    sign = jnp.where(flip == 1, 1.0, -1.0)
    rate = sign * OPACITY
    lx, ly, lz = (0.65 * v for v in LIGHT)
    lane = lax.broadcasted_iota(jnp.int32, (SUB, LANES), 1)
    first_lane = lane == 0
    last_lane = lane == LANES - 1
    base = (position * cells).astype(jnp.float32)
    step = 1.0 / (cells * count)
    start = (base + 0.5) * step
    finish = (base + (cells - 0.5)) * step
    h_first = jnp.where(flip == 1, 1.0 - start, start)
    h_last = jnp.where(flip == 1, 1.0 - finish, finish)
    delta = jnp.where(flip == 1, -step, step)

    def poly(c, t):
        return c[0] + t * (c[1] + t * (c[2] + t * c[3]))

    def arrive(b):
        for j in range(own + 2):
            copy(b, j).wait()
        at = pl.ds(SUB + b * SUB, SUB)

        @pl.when(first == 0)
        def _():
            for z in range(cells):
                field[z, 0, at, :] = jnp.zeros((SUB, LANES), jnp.int32)

        @pl.when(first + own == tiles)
        def _():
            for z in range(cells):
                field[z, own + 1, at, :] = jnp.zeros((SUB, LANES), jnp.int32)

    arrive(0)

    def block(b, carry):
        @pl.when(b + 1 < blocks)
        def _():
            arrive(b + 1)

        r = pl.multiple_of(b * SUB, SUB)
        for j in range(1, own + 1):
            column(r, j)
        return carry

    def column(r, j):
        at = pl.ds(r + SUB, SUB)
        zero = jnp.zeros((SUB, LANES), jnp.float32)
        tau = zero
        factor = jnp.ones((SUB, LANES), jnp.float32)
        between = zero
        sums = [zero] * 6
        below = zlo_f[j - 1, pl.ds(r, SUB), :]
        raw = field[0, j, at, :]
        here = raw.astype(jnp.float32) - CENTRE
        for z in range(cells):
            if z + 1 < cells:
                raw_above = field[z + 1, j, at, :]
                above = raw_above.astype(jnp.float32) - CENTRE
            else:
                raw_above = raw
                above = zhi_f[j - 1, pl.ds(r, SUB), :]
            left = pltpu.roll(jnp.where(last_lane, field[z, j - 1, at, :], raw), 1, 1)
            right = pltpu.roll(jnp.where(first_lane, field[z, j + 1, at, :], raw), LANES - 1, 1)
            gx = (right - left).astype(jnp.float32)
            up = field[z, j, pl.ds(r + SUB + 1, SUB), :]
            gy = (up - field[z, j, pl.ds(r + SUB - 1, SUB), :]).astype(jnp.float32)
            gz = above - below
            norm = lax.rsqrt(gx * gx + gy * gy + (gz * gz + 255.0 * 255.0))
            shade = 0.35 + jnp.abs((lx * gx + ly * gy + lz * gz) * norm)
            tau = tau + jnp.log2(1.0 + jnp.exp2(poly(coeffs[0], here)))
            following = jnp.exp2(rate * tau)
            weight = following - factor
            factor = following
            if z < cells - 1:
                between = between + following
            tilt = weight * norm
            lit = weight * shade
            terms = [lit * (1.0 / (1.0 + jnp.exp2(poly(coeffs[k], here)))) for k in (1, 2, 3)]
            terms += [tilt * gx, tilt * gy, tilt * gz]
            sums = [s + t for s, t in zip(sums, terms)]
            below, here, raw = here, above, raw_above
        inverse = 1.0 / factor
        flipped = flip == 1
        scale = jnp.where(flipped, inverse, -1.0)
        out = pl.ds(r, SUB)
        for k in range(3):
            out_ref[k, j - 1, out, :] = sums[k] * scale
            out_ref[k + 5, j - 1, out, :] = sums[k + 3] * scale
        out_ref[3, j - 1, out, :] = 1.0 - jnp.where(flipped, inverse, factor)
        out_ref[4, j - 1, out, :] = (h_last * factor - h_first - delta * between) * scale

    lax.fori_loop(0, blocks, block, 0)


def integrate(place, count, view_flip, tf_coeff, density, zlo, zhi, ylo, yhi):
    cells, rows, width = density.shape
    own = width // LANES // count
    smem = pl.BlockSpec(memory_space=pltpu.SMEM)
    vmem = pl.BlockSpec(memory_space=pltpu.VMEM)
    voxels = cells * rows * own * LANES
    return pl.pallas_call(
        functools.partial(integrate_kernel, place, own),
        out_shape=jax.ShapeDtypeStruct((8, own, rows, LANES), jnp.float32),
        in_specs=[smem, smem, pl.BlockSpec(memory_space=pl.ANY), vmem, vmem, vmem, vmem],
        out_specs=vmem,
        scratch_shapes=[
            pltpu.VMEM((cells, own + 2, rows + 2 * SUB, LANES), jnp.int32),
            pltpu.VMEM((own, rows, LANES), jnp.float32),
            pltpu.VMEM((own, rows, LANES), jnp.float32),
            pltpu.SemaphoreType.DMA((rows // SUB, own + 2)),
        ],
        compiler_params=pltpu.CompilerParams(vmem_limit_bytes=24 << 20),
        cost_estimate=pl.CostEstimate(
            flops=70 * voxels, transcendentals=10 * voxels, bytes_accessed=8 * voxels
        ),
        name="integrate",
    )(view_flip, tf_coeff, density, zlo, zhi, ylo, yhi)


def shade_kernel(
    core_ref, left_ref, right_ref, top_ref, bottom_ref, out_ref, planes, feats, buf_a, buf_b, acc
):
    _, tiles, rows, _ = core_ref.shape
    blocks = rows // SUB
    halves = blocks // 4
    cols = tiles * LANES
    for k in range(8):
        for t in (0, tiles + 1):
            planes[k, t] = jnp.zeros((rows + 2 * SUB, LANES), jnp.float32)
        planes[k, 0, SUB : SUB + rows, LANES - RADIUS : LANES] = left_ref[k]
        planes[k, tiles + 1, SUB : SUB + rows, 0:RADIUS] = right_ref[k]
        for j in range(tiles):
            planes[k, j + 1, SUB : SUB + rows, :] = core_ref[k, j]
        for ref, start in ((top_ref, 0), (bottom_ref, SUB + rows)):
            planes[k, 0, start : start + SUB, LANES - RADIUS : LANES] = ref[k, :, 0:RADIUS]
            planes[k, tiles + 1, start : start + SUB, 0:RADIUS] = ref[
                k, :, cols + RADIUS : cols + 2 * RADIUS
            ]
            for j in range(tiles):
                planes[k, j + 1, start : start + SUB, :] = ref[
                    k, :, RADIUS + j * LANES : RADIUS + (j + 1) * LANES
                ]

    row_blocks = blocks + 2

    def features(index, carry):
        t = index // row_blocks
        at = pl.ds(pl.multiple_of((index % row_blocks) * SUB, SUB), SUB)
        red, green, blue, alpha, depth, nx, ny, nz = [planes[k, t, at, :] for k in range(8)]
        facing = jnp.maximum(LIGHT[0] * nx + LIGHT[1] * ny + LIGHT[2] * nz, 0.0)
        lit = 0.4 + 0.6 * facing
        own = (DEPTH_W * LOG2E) * depth * depth + (NORMAL_W * LOG2E) * (nx * nx + ny * ny + nz * nz)
        feats[0, t, at, :] = jnp.log2(jnp.maximum(alpha, 1e-37)) - own
        feats[1, t, at, :] = depth
        feats[2, t, at, :] = nx
        feats[3, t, at, :] = ny
        feats[4, t, at, :] = nz
        feats[5, t, at, :] = red * lit
        feats[6, t, at, :] = green * lit
        feats[7, t, at, :] = blue * lit
        return carry

    lax.fori_loop(0, (tiles + 2) * row_blocks, features, 0)
    lane = lax.broadcasted_iota(jnp.int32, (SUB, LANES), 1)


    def shift_setup(index):
        offset = index - RADIUS
        run = offset.astype(jnp.float32)
        spread = -(SPATIAL * LOG2E) * run * run
        border = jnp.where(offset < 0, LANES + offset, offset)
        amount = jnp.where(offset > 0, LANES - offset, -offset)
        below = lane < border
        take_other = (below & (offset >= 0)) | (jnp.logical_not(below) & (offset < 0))
        return jnp.where(offset < 0, 0, 2), amount, take_other, spread

    def moved(setup, k, j, blk):
        other, amount, take_other, spread = setup
        at = pl.ds(blk * SUB, SUB)
        mixed = jnp.where(take_other, feats[k, j + other, at, :], feats[k, j + 1, at, :])
        m = pltpu.roll(mixed, amount, 1)
        return m + spread if k == 0 else m

    def shift(index, buf, j, blk):
        s = shift_setup(index)
        at = pl.ds(pl.multiple_of(blk * SUB, SUB), SUB)
        for k in range(8):
            buf[k, j, at, :] = moved(s, k, j, blk)

    for j in range(tiles):
        for k in range(4):
            acc[k, j] = jnp.zeros((rows, LANES), jnp.float32)

    def shift_all(index, buf):
        def one(t, carry):
            shift(index, buf, t // row_blocks, t % row_blocks)
            return carry

        lax.fori_loop(0, tiles * row_blocks, one, 0)

    share = -(-row_blocks // halves)

    def taps(buf, next_index, next_buf):
        pending = []
        items = []
        if next_buf is not None:
            setup = shift_setup(next_index)
            items = [(k, jj, b) for jj in range(tiles) for b in range(row_blocks) for k in range(8)]

        def pump(force=False):
            for _ in range(2):
                if items:
                    k, jj, b = items.pop(0)
                    pending.append((moved(setup, k, jj, b), k, jj, b))
            while len(pending) > (0 if force else 8):
                v, k, jj, b = pending.pop(0)
                next_buf[k, jj, pl.ds(b * SUB, SUB), :] = v

        def one(t, carry):
            j = t // halves
            half = t % halves
            first = half * 4
            own = []
            for i in range(4):
                rows_at = pl.ds(SUB + first + i, SUB, stride=blocks)
                depth = feats[1, j + 1, rows_at, :] * (2.0 * DEPTH_W * LOG2E)
                normal = [
                    feats[k, j + 1, rows_at, :] * (2.0 * NORMAL_W * LOG2E) for k in (2, 3, 4)
                ]
                own.append([depth] + normal)
            sums = [
                [acc[k, j, pl.ds(first + i, SUB, stride=blocks), :] for k in range(4)]
                for i in range(4)
            ]
            for near in range(-RADIUS, 4 + RADIUS):
                q = [
                    buf[k, j, pl.ds(SUB + first + near, SUB, stride=blocks), :] for k in range(8)
                ]
                pump()
                for i in range(4):
                    dy = near - i
                    if abs(dy) > RADIUS:
                        continue
                    p = own[i]
                    power = (q[0] + p[0] * q[1]) + (p[1] * q[2] + p[2] * q[3])
                    power = power + (p[3] * q[4] - SPATIAL * LOG2E * dy * dy)
                    weight = jnp.exp2(power)
                    s = sums[i]
                    sums[i] = [
                        s[0] + weight * q[5],
                        s[1] + weight * q[6],
                        s[2] + weight * q[7],
                        s[3] + weight,
                    ]
            for i in range(4):
                for k in range(4):
                    acc[k, j, pl.ds(first + i, SUB, stride=blocks), :] = sums[i][k]
            return carry

        for t in range(tiles*halves): one(t,0)
        while items or pending: pump(not items)

    shift_all(jnp.int32(0), buf_a)

    def pair(step, carry):
        taps(buf_a, 2 * step + 1, buf_b)
        taps(buf_b, 2 * step + 2, buf_a)
        return carry

    lax.fori_loop(0, RADIUS, pair, 0)
    taps(buf_a, None, None)

    for j in range(tiles):
        for b in range(blocks):
            at = pl.ds(b * SUB, SUB)
            inner = pl.ds(SUB + b * SUB, SUB)
            depth, nx, ny, nz = [feats[k, j + 1, inner, :] for k in (1, 2, 3, 4)]
            own = (DEPTH_W * LOG2E) * depth * depth + (NORMAL_W * LOG2E) * (
                nx * nx + ny * ny + nz * nz
            )
            level = jnp.exp2(-own)
            scale = level / (1.0 + level * acc[3, j, at, :])
            for k in range(3):
                out_ref[k, at, pl.ds(j * LANES, LANES)] = acc[k, j, at, :] * scale


def shade(core, left, right, top, bottom):
    _, tiles, rows, _ = core.shape
    vmem = pl.BlockSpec(memory_space=pltpu.VMEM)
    wide = (8, tiles + 2, rows + 2 * SUB, LANES)
    moved = (8, tiles, rows + 2 * SUB, LANES)
    return pl.pallas_call(
        shade_kernel,
        out_shape=jax.ShapeDtypeStruct((3, rows, tiles * LANES), jnp.float32),
        in_specs=[vmem] * 5,
        out_specs=vmem,
        scratch_shapes=[
            pltpu.VMEM(wide, jnp.float32),
            pltpu.VMEM(wide, jnp.float32),
            pltpu.VMEM(moved, jnp.float32),
            pltpu.VMEM(moved, jnp.float32),
            pltpu.VMEM((4, tiles, rows, LANES), jnp.float32),
        ],
        compiler_params=pltpu.CompilerParams(vmem_limit_bytes=32 << 20),
        name="shade",
    )(core, left, right, top, bottom)


def reverse_bits(value, rounds):
    result = 0
    for level in range(rounds):
        result = result * 2 + (value >> level) % 2
    return result


def over(kept, partner, kept_leads):
    front = jnp.where(kept_leads, kept, partner)
    back = jnp.where(kept_leads, partner, kept)
    return front + (1.0 - front[3:4]) * back


def per_device(density, view_flip, tf_coeff):
    cells, rows, width = density.shape
    count = lax.axis_size("depth")
    position = lax.axis_index("depth")
    flipped = view_flip[0]
    rounds = count.bit_length() - 1
    high = count // 4
    first_plane, last_plane, first_line, last_line = edges(density)
    up, down = shifts("depth")
    zlo = lax.ppermute(last_plane, "depth", up)
    zhi = lax.ppermute(first_plane, "depth", down)
    up, down = shifts("tile")
    ylo = lax.ppermute(last_line, "tile", up)
    yhi = lax.ppermute(first_line, "tile", down)

    def quarter(core_bit, chip_bit, flip):
        parts = [
            integrate(
                (core_bit, chip_bit, h), count, flip, tf_coeff, density, zlo, zhi, ylo, yhi
            )
            for h in range(high)
        ]
        return jnp.stack(parts, axis=1)

    leads = [position // 2**level % 2 == flipped for level in range(rounds)]
    far_given = quarter(1, 1, view_flip)
    far_given, flip = lax.optimization_barrier((far_given, view_flip))
    far_partner = swapped(far_given, "depth", 0)
    far_kept = quarter(0, 1, flip)
    far = over(far_kept, far_partner, leads[0])
    far, flip = lax.optimization_barrier((far, flip))
    chip_partner = swapped(far, "depth", 1)
    near_given = quarter(1, 0, flip)
    near_given, flip = lax.optimization_barrier((near_given, flip))
    near_partner = swapped(near_given, "depth", 0)
    near_kept = quarter(0, 0, flip)
    current = over(over(near_kept, near_partner, leads[0]), chip_partner, leads[1])
    for level in range(2, rounds):
        half = current.shape[1] // 2
        order = [reverse_bits(place, rounds - 2) for place in range(high)]
        if level == 2:
            current = jnp.concatenate([current[:, p : p + 1] for p in order], axis=1)
        upper = position // 2**level % 2
        kept = lax.dynamic_slice_in_dim(current, upper * half, half, 1)
        given = lax.dynamic_slice_in_dim(current, (1 - upper) * half, half, 1)
        current = over(kept, swapped(given, "depth", level), leads[level])
    core = current[:, 0]
    own = core.shape[1]
    up, down = shifts("depth")
    left = lax.ppermute(core[:, -1, :, LANES - RADIUS :], "depth", up)
    right = lax.ppermute(core[:, 0, :, :RADIUS], "depth", down)
    up, down = shifts("tile")

    def edge(start):
        pieces = [left[:, start : start + RADIUS]]
        pieces += [core[:, j, start : start + RADIUS] for j in range(own)]
        pieces += [right[:, start : start + RADIUS]]
        return jnp.concatenate(pieces, axis=2)

    top = lax.ppermute(edge(rows - RADIUS), "tile", up)
    bottom = lax.ppermute(edge(0), "tile", down)
    return shade(core, left, right, top, bottom)


def solution(mesh):
    in_specs = (P("depth", "tile", None), P("tile"), P())
    out_specs = P(None, "tile", "depth")
    return jax.shard_map(
        per_device, mesh=mesh, in_specs=in_specs, out_specs=out_specs, check_vma=False
    )
```

```python
import functools
import math

import jax
import jax.numpy as jnp
from jax import lax
from jax.experimental import pallas as pl
from jax.experimental.pallas import tpu as pltpu
from jax.sharding import PartitionSpec as P

RADIUS = 8
LANES = 128
SUB = 8
LOG2E = math.log2(math.e)
OPACITY = 0.008
LIGHT = (0.48, 0.6, 0.64)
SPATIAL = 1.0 / 72.0
DEPTH_W = 20.0
NORMAL_W = 2.0
CENTRE = 127.5
AHEAD = 8


def shifts(axis):
    count = lax.axis_size(axis)
    up = [(i, i + 1) for i in range(count - 1)]
    return up, [(j, i) for i, j in up]


def swapped(block, axis, stride):
    count = lax.axis_size(axis)
    route = []
    for low in range(count):
        high = low | 1 << stride
        if high != low and high < count:
            route += [(low, high), (high, low)]
    return lax.ppermute(block, axis, route)


def edges_kernel(density_ref, zlo_ref, zhi_ref, ylo_ref, yhi_ref, planes, bands, lines, sems):
    cells, rows, width = density_ref.shape
    tiles = width // LANES
    copies = []
    for side in range(2):
        copies.append(
            pltpu.make_async_copy(
                density_ref.at[side * (cells - 1)], planes.at[side], sems.at[2 * side]
            )
        )
        copies.append(
            pltpu.make_async_copy(
                density_ref.at[:, side * (rows - SUB) : side * (rows - SUB) + SUB, :],
                bands.at[side],
                sems.at[2 * side + 1],
            )
        )
    for copy in copies:
        copy.start()
    for copy in copies:
        copy.wait()
    zlo_ref[...] = planes[0].astype(jnp.float32).astype(jnp.bfloat16)
    zhi_ref[...] = planes[1].astype(jnp.float32).astype(jnp.bfloat16)
    for side, ref in ((0, ylo_ref), (1, yhi_ref)):
        row = side * (SUB - 1)
        for z in range(cells):
            lines[z : z + 1, :] = bands[side, z, row : row + 1, :].astype(jnp.float32)
        ref[...] = lines[...].astype(jnp.bfloat16)


def edges(density):
    cells, rows, width = density.shape
    vmem = pl.BlockSpec(memory_space=pltpu.VMEM)
    plane = jax.ShapeDtypeStruct((rows, width), jnp.bfloat16)
    line = jax.ShapeDtypeStruct((cells, width), jnp.bfloat16)
    return pl.pallas_call(
        edges_kernel,
        out_shape=(plane, plane, line, line),
        in_specs=[pl.BlockSpec(memory_space=pl.ANY)],
        out_specs=[vmem] * 4,
        scratch_shapes=[
            pltpu.VMEM((2, rows, width), jnp.int32),
            pltpu.VMEM((2, cells, SUB, width), jnp.int32),
            pltpu.VMEM((cells, width), jnp.float32),
            pltpu.SemaphoreType.DMA((4,)),
        ],
        compiler_params=pltpu.CompilerParams(vmem_limit_bytes=52 << 20),
        name="edges",
    )(density)


def integrate_kernel(
    place, own, flip_ref, coeff_ref, density_ref, zlo_ref, zhi_ref, ylo_ref, yhi_ref, token_ref,
    out_ref, field, zlo_f, zhi_f, sems,
):
    cells, rows, width = density_ref.shape
    tiles = width // LANES
    blocks = rows // SUB
    count = tiles // own
    position = lax.axis_index("depth")
    c, y = position % 2, position // 2 % 2
    first = (lax.rem(c + place[0], 2) + 2 * lax.rem(y + place[1], 2) + 4 * place[2]) * own
    sources = [jnp.maximum(first - 1, 0)]
    sources += [first + j for j in range(own)]
    sources += [jnp.minimum(first + own, tiles - 1)]

    def copy(b, j):
        start = pl.multiple_of(sources[j] * LANES, LANES)
        return pltpu.make_async_copy(
            density_ref.at[:, pl.ds(b * SUB, SUB), pl.ds(start, LANES)],
            field.at[:, j, pl.ds(SUB + b * SUB, SUB), :],
            sems.at[b, j],
        )

    for b in range(blocks):
        for j in range(own + 2):
            copy(b, j).start()
    flip = flip_ref[0]
    for j in range(own):
        cols = pl.ds(pl.multiple_of((first + j) * LANES, LANES), LANES)
        zlo_f[j] = zlo_ref[:, cols].astype(jnp.float32) - CENTRE
        zhi_f[j] = zhi_ref[:, cols].astype(jnp.float32) - CENTRE
        top = ylo_ref[:, cols].astype(jnp.float32).astype(jnp.int32)
        bottom = yhi_ref[:, cols].astype(jnp.float32).astype(jnp.int32)
        for z in range(cells):
            field[z, j + 1, SUB - 1 : SUB, :] = top[z : z + 1]
            field[z, j + 1, SUB + rows : SUB + rows + 1, :] = bottom[z : z + 1]

    coeffs = []
    for row in range(4):
        scale = LOG2E if row == 0 else -LOG2E
        coeffs.append([coeff_ref[row, k] * (scale / CENTRE**k) for k in range(4)])
    sign = jnp.where(flip == 1, 1.0, -1.0)
    rate = sign * OPACITY
    lx, ly, lz = (0.65 * v for v in LIGHT)
    lane = lax.broadcasted_iota(jnp.int32, (SUB, LANES), 1)
    first_lane = lane == 0
    last_lane = lane == LANES - 1
    base = (position * cells).astype(jnp.float32)
    step = 1.0 / (cells * count)
    start = (base + 0.5) * step
    finish = (base + (cells - 0.5)) * step
    h_first = jnp.where(flip == 1, 1.0 - start, start)
    h_last = jnp.where(flip == 1, 1.0 - finish, finish)
    delta = jnp.where(flip == 1, -step, step)

    def poly(c, t):
        return c[0] + t * (c[1] + t * (c[2] + t * c[3]))

    def arrive(b):
        for j in range(own + 2):
            copy(b, j).wait()
        at = pl.ds(SUB + b * SUB, SUB)

        @pl.when(first == 0)
        def _():
            for z in range(cells):
                field[z, 0, at, :] = jnp.zeros((SUB, LANES), jnp.int32)

        @pl.when(first + own == tiles)
        def _():
            for z in range(cells):
                field[z, own + 1, at, :] = jnp.zeros((SUB, LANES), jnp.int32)

    arrive(0)

    def block(b, carry):
        @pl.when(b + 1 < blocks)
        def _():
            arrive(b + 1)

        r = pl.multiple_of(b * SUB, SUB)
        for j in range(1, own + 1):
            column(r, j)
        return carry

    def column(r, j):
        at = pl.ds(r + SUB, SUB)
        zero = jnp.zeros((SUB, LANES), jnp.float32)
        tau = zero
        factor = jnp.ones((SUB, LANES), jnp.float32)
        between = zero
        sums = [zero] * 6
        below = zlo_f[j - 1, pl.ds(r, SUB), :]
        raw = field[0, j, at, :]
        here = raw.astype(jnp.float32) - CENTRE
        for z in range(cells):
            if z + 1 < cells:
                raw_above = field[z + 1, j, at, :]
                above = raw_above.astype(jnp.float32) - CENTRE
            else:
                raw_above = raw
                above = zhi_f[j - 1, pl.ds(r, SUB), :]
            left = pltpu.roll(jnp.where(last_lane, field[z, j - 1, at, :], raw), 1, 1)
            right = pltpu.roll(jnp.where(first_lane, field[z, j + 1, at, :], raw), LANES - 1, 1)
            gx = (right - left).astype(jnp.float32)
            up = field[z, j, pl.ds(r + SUB + 1, SUB), :]
            gy = (up - field[z, j, pl.ds(r + SUB - 1, SUB), :]).astype(jnp.float32)
            gz = above - below
            norm = lax.rsqrt(gx * gx + gy * gy + (gz * gz + 255.0 * 255.0))
            shade = 0.35 + jnp.abs((lx * gx + ly * gy + lz * gz) * norm)
            tau = tau + jnp.log2(1.0 + jnp.exp2(poly(coeffs[0], here)))
            following = jnp.exp2(rate * tau)
            weight = following - factor
            factor = following
            if z < cells - 1:
                between = between + following
            tilt = weight * norm
            lit = weight * shade
            terms = [lit * (1.0 / (1.0 + jnp.exp2(poly(coeffs[k], here)))) for k in (1, 2, 3)]
            terms += [tilt * gx, tilt * gy, tilt * gz]
            sums = [s + t for s, t in zip(sums, terms)]
            below, here, raw = here, above, raw_above
        inverse = 1.0 / factor
        flipped = flip == 1
        scale = jnp.where(flipped, inverse, -1.0)
        out = pl.ds(r, SUB)
        for k in range(3):
            out_ref[k, j - 1, out, :] = sums[k] * scale
            out_ref[k + 5, j - 1, out, :] = sums[k + 3] * scale
        out_ref[3, j - 1, out, :] = 1.0 - jnp.where(flipped, inverse, factor)
        out_ref[4, j - 1, out, :] = (h_last * factor - h_first - delta * between) * scale

    lax.fori_loop(0, blocks, block, 0)


def integrate(place, count, view_flip, tf_coeff, density, zlo, zhi, ylo, yhi, token):
    cells, rows, width = density.shape
    own = width // LANES // count
    smem = pl.BlockSpec(memory_space=pltpu.SMEM)
    vmem = pl.BlockSpec(memory_space=pltpu.VMEM)
    anywhere = pl.BlockSpec(memory_space=pl.ANY)
    voxels = cells * rows * own * LANES
    return pl.pallas_call(
        functools.partial(integrate_kernel, place, own),
        out_shape=jax.ShapeDtypeStruct((8, own, rows, LANES), jnp.float32),
        in_specs=[smem, smem, anywhere, vmem, vmem, vmem, vmem, anywhere],
        out_specs=vmem,
        scratch_shapes=[
            pltpu.VMEM((cells, own + 2, rows + 2 * SUB, LANES), jnp.int32),
            pltpu.VMEM((own, rows, LANES), jnp.float32),
            pltpu.VMEM((own, rows, LANES), jnp.float32),
            pltpu.SemaphoreType.DMA((rows // SUB, own + 2)),
        ],
        compiler_params=pltpu.CompilerParams(vmem_limit_bytes=52 << 20),
        cost_estimate=pl.CostEstimate(
            flops=70 * voxels, transcendentals=0, bytes_accessed=8 * voxels
        ),
        name="integrate",
    )(view_flip, tf_coeff, density, zlo, zhi, ylo, yhi, token)


def shade_kernel(inner, core_ref, halo_ref, *rest):
    if inner:
        out_ref, planes, feats, buf_a, buf_b, acc = rest
    else:
        top_ref, bottom_ref, done_ref, out_ref, planes, feats, buf_a, buf_b, acc = rest
    _, tiles, rows, _ = core_ref.shape
    blocks = rows // SUB
    chosen = list(range(1, blocks - 1)) if inner else [0, blocks - 1]
    needed = sorted({n for b in chosen for n in (b - 1, b, b + 1)})

    def at(n):
        return pl.ds(SUB + n * SUB, SUB)

    for k in range(8):
        for n in needed:
            for t in (0, tiles + 1):
                planes[k, t, at(n), :] = jnp.zeros((SUB, LANES), jnp.float32)
            if 0 <= n < blocks:
                here = slice(n * SUB, n * SUB + SUB)
                side = halo_ref[here, :]
                for j in range(tiles):
                    planes[k, j + 1, at(n), :] = core_ref[k, j, here, :]
            else:
                ref = top_ref if n < 0 else bottom_ref
                side = ref[8 * tiles]
                for j in range(tiles):
                    planes[k, j + 1, at(n), :] = ref[k * tiles + j]
            left = side[:, RADIUS * k : RADIUS * k + RADIUS]
            right = side[:, RADIUS * (8 + k) : RADIUS * (9 + k)]
            planes[k, 0, at(n), LANES - RADIUS : LANES] = left
            planes[k, tiles + 1, at(n), 0:RADIUS] = right

    def features(t, carry):
        for n in needed:
            red, green, blue, alpha, depth, nx, ny, nz = [planes[k, t, at(n), :] for k in range(8)]
            facing = jnp.maximum(LIGHT[0] * nx + LIGHT[1] * ny + LIGHT[2] * nz, 0.0)
            lit = 0.4 + 0.6 * facing
            level = (DEPTH_W * LOG2E) * depth * depth
            level = level + (NORMAL_W * LOG2E) * (nx * nx + ny * ny + nz * nz)
            feats[0, t, at(n), :] = jnp.log2(jnp.maximum(alpha, 1e-37)) - level
            feats[1, t, at(n), :] = depth
            feats[2, t, at(n), :] = nx
            feats[3, t, at(n), :] = ny
            feats[4, t, at(n), :] = nz
            feats[5, t, at(n), :] = red * lit
            feats[6, t, at(n), :] = green * lit
            feats[7, t, at(n), :] = blue * lit
        return carry

    lax.fori_loop(0, tiles + 2, features, 0)
    lane = lax.broadcasted_iota(jnp.int32, (SUB, LANES), 1)

    def shift_setup(index):
        offset = index - RADIUS
        run = offset.astype(jnp.float32)
        spread = -(SPATIAL * LOG2E) * run * run
        border = jnp.where(offset < 0, LANES + offset, offset)
        amount = jnp.where(offset > 0, LANES - offset, -offset)
        below = lane < border
        take_other = (below & (offset >= 0)) | (jnp.logical_not(below) & (offset < 0))
        return jnp.where(offset < 0, 0, 2), amount, take_other, spread

    def moved(setup, k, j, n):
        other, amount, take_other, spread = setup
        mixed = jnp.where(take_other, feats[k, j + other, at(n), :], feats[k, j + 1, at(n), :])
        result = pltpu.roll(mixed, amount, 1)
        return result + spread if k == 0 else result

    def first_shift(k, carry):
        other, amount, take_other, spread = shift_setup(jnp.int32(0))
        for j in range(tiles):
            for n in needed:
                mixed = jnp.where(take_other, feats[k, j + other, at(n), :], feats[k, j + 1, at(n), :])
                result = pltpu.roll(mixed, amount, 1)
                buf_a[k, j, at(n), :] = result + jnp.where(k == 0, spread, 0.0)
        return carry

    lax.fori_loop(0, 8, first_shift, 0)
    for k in range(4):
        for j in range(tiles):
            for b in chosen:
                acc[k, j, at(b), :] = jnp.zeros((SUB, LANES), jnp.float32)

    offsets = sorted({o for b in chosen for o in range(SUB * b - RADIUS, SUB * b + RADIUS + 1)})

    def taps(buf, next_index, next_buf):
        pending, items = [], []
        if next_buf is not None:
            setup = shift_setup(next_index)
            items = [(k, j, n) for j in range(tiles) for n in needed for k in range(8)]
        pace = -(-len(items) // (len(offsets) * tiles))

        def pump(last=False):
            for _ in range(pace):
                if items:
                    pending.append((moved(setup, *items[0]),) + items.pop(0))
            while len(pending) > (0 if last else AHEAD):
                value, k, j, n = pending.pop(0)
                next_buf[k, j, at(n), :] = value

        for j in range(tiles):
            own, sums = {}, {}
            for o in offsets:
                pump()
                q = [buf[k, j, pl.ds(SUB + o, SUB), :] for k in range(8)]
                for b in chosen:
                    dy = o - SUB * b
                    if abs(dy) > RADIUS:
                        continue
                    if dy == -RADIUS:
                        own[b] = [feats[1, j + 1, at(b), :] * (2.0 * DEPTH_W * LOG2E)]
                        own[b] += [
                            feats[k, j + 1, at(b), :] * (2.0 * NORMAL_W * LOG2E) for k in (2, 3, 4)
                        ]
                        sums[b] = [acc[k, j, at(b), :] for k in range(4)]
                    p, s = own[b], sums[b]
                    power = (q[0] + p[0] * q[1]) + (p[1] * q[2] + p[2] * q[3])
                    power = power + (p[3] * q[4] - SPATIAL * LOG2E * dy * dy)
                    weight = jnp.exp2(power)
                    sums[b] = [s[k] + weight * q[5 + k] for k in range(3)] + [s[3] + weight]
                    if dy == RADIUS:
                        for k in range(4):
                            acc[k, j, at(b), :] = sums[b][k]
        while items or pending:
            pump(not items)

    def pair(step, carry):
        taps(buf_a, 2 * step + 1, buf_b)
        taps(buf_b, 2 * step + 2, buf_a)
        return carry

    lax.fori_loop(0, RADIUS, pair, 0)
    taps(buf_a, None, None)

    if not inner:
        for k in range(3):
            out_ref[k, SUB : rows - SUB, :] = done_ref[k, SUB : rows - SUB, :]
    for j in range(tiles):
        for b in chosen:
            depth, nx, ny, nz = [feats[k, j + 1, at(b), :] for k in (1, 2, 3, 4)]
            own = (DEPTH_W * LOG2E) * depth * depth
            own = own + (NORMAL_W * LOG2E) * (nx * nx + ny * ny + nz * nz)
            level = jnp.exp2(-own)
            scale = level / (1.0 + level * acc[3, j, at(b), :])
            for k in range(3):
                out_ref[k, b * SUB : b * SUB + SUB, j * LANES : (j + 1) * LANES] = (
                    acc[k, j, at(b), :] * scale
                )


def shade(inner, core, *rest):
    _, tiles, rows, _ = core.shape
    vmem = pl.BlockSpec(memory_space=pltpu.VMEM)
    wide = (8, tiles + 2, rows + 2 * SUB, LANES)
    moved = (8, tiles, rows + 2 * SUB, LANES)
    part = rows - 2 * SUB if inner else 2 * SUB
    work = part * tiles * LANES * (2 * RADIUS + 1) ** 2
    return pl.pallas_call(
        functools.partial(shade_kernel, inner),
        out_shape=jax.ShapeDtypeStruct((3, rows, tiles * LANES), jnp.float32),
        in_specs=[vmem] * (1 + len(rest)),
        out_specs=vmem,
        scratch_shapes=[
            pltpu.VMEM(wide, jnp.float32),
            pltpu.VMEM(wide, jnp.float32),
            pltpu.VMEM(moved, jnp.float32),
            pltpu.VMEM(moved, jnp.float32),
            pltpu.VMEM((4, tiles, rows + 2 * SUB, LANES), jnp.float32),
        ],
        compiler_params=pltpu.CompilerParams(vmem_limit_bytes=24 << 20),
        cost_estimate=pl.CostEstimate(
            flops=16 * work, transcendentals=work, bytes_accessed=8 * rows * tiles * LANES * 4
        ),
        name="shade_inner" if inner else "shade_outer",
    )(core, *rest)


def compose_kernel(base, pieces, mode, leads_ref, *refs):
    images, at_ref = [], 0
    for n in pieces:
        images.append(refs[at_ref : at_ref + n])
        at_ref += n
    outs = refs[at_ref:]
    _, tiles, rows, _ = outs[0].shape
    halves = outs if mode == "halves" else outs[:1]

    def plane(parts, k):
        size = 8 // len(parts)
        return parts[k // size], k % size

    def one(t, carry):
        j = t // (rows // SUB)
        at = pl.ds(pl.multiple_of(t % (rows // SUB) * SUB, SUB), SUB)

        def read(parts):
            found = [plane(parts, k) for k in range(8)]
            return [ref[k, j, at, :] for ref, k in found]

        current = read(images[0])
        for level, parts in enumerate(images[1:]):
            other = read(parts)
            leads = leads_ref[base + level] == 1
            share = jnp.where(leads, 1.0, 1.0 - other[3])
            other_share = jnp.where(leads, 1.0 - current[3], 1.0)
            current = [c * share + o * other_share for c, o in zip(current, other)]
        for k in range(8):
            ref, kk = plane(halves, k)
            ref[kk, j, at, :] = current[k]
        return carry

    lax.fori_loop(0, tiles * (rows // SUB), one, 0)
    if mode == "borders":
        out_ref, last_ref, first_ref = outs
        last_ref[...] = jnp.zeros((rows, LANES), jnp.float32)
        first_ref[...] = jnp.zeros((rows, LANES), jnp.float32)
        for k in range(8):
            last_ref[:, RADIUS * k : RADIUS * k + RADIUS] = out_ref[
                k, tiles - 1, :, LANES - RADIUS : LANES
            ]
            first_ref[:, RADIUS * (8 + k) : RADIUS * (9 + k)] = out_ref[k, 0, :, 0:RADIUS]


def compose(base, mode, leads, *images):
    images = [i if isinstance(i, (tuple, list)) else (i,) for i in images]
    _, tiles, rows, _ = images[0][0].shape
    smem = pl.BlockSpec(memory_space=pltpu.SMEM)
    vmem = pl.BlockSpec(memory_space=pltpu.VMEM)
    whole = jax.ShapeDtypeStruct((8, tiles, rows, LANES), jnp.float32)
    half = jax.ShapeDtypeStruct((4, tiles, rows, LANES), jnp.float32)
    border = jax.ShapeDtypeStruct((rows, LANES), jnp.float32)
    outs = {"plain": (whole,), "halves": (half, half), "borders": (whole, border, border)}[mode]
    parts = [p for image in images for p in image]
    return pl.pallas_call(
        functools.partial(compose_kernel, base, [len(i) for i in images], mode),
        out_shape=outs,
        in_specs=[smem] + [vmem] * len(parts),
        out_specs=[vmem] * len(outs),
        compiler_params=pltpu.CompilerParams(vmem_limit_bytes=8 << 20),
        cost_estimate=pl.CostEstimate(
            flops=0, transcendentals=0, bytes_accessed=32 * tiles * rows * LANES
        ),
        name="compose",
    )(leads, *parts)


def reverse_bits(value, rounds):
    result = 0
    for level in range(rounds):
        result = result * 2 + (value >> level) % 2
    return result


def per_device(density, view_flip, tf_coeff):
    cells, rows, width = density.shape
    count = lax.axis_size("depth")
    position = lax.axis_index("depth")
    flipped = view_flip[0]
    rounds = count.bit_length() - 1
    high = count // 4
    first_plane, last_plane, first_line, last_line = edges(density)
    up, down = shifts("depth")
    zlo = lax.ppermute(last_plane, "depth", up)
    zhi = lax.ppermute(first_plane, "depth", down)
    up, down = shifts("tile")
    ylo = lax.ppermute(last_line, "tile", up)
    yhi = lax.ppermute(first_line, "tile", down)

    def quarter(core_bit, chip_bit, token):
        parts = [
            integrate(
                (core_bit, chip_bit, h), count, view_flip, tf_coeff, density, zlo, zhi, ylo, yhi, token
            )
            for h in range(high)
        ]
        return parts[0] if high == 1 else jnp.concatenate(parts, axis=1)

    bits = [position // 2**level % 2 for level in range(rounds)]
    leads = jnp.stack([bit == flipped for bit in bits]).astype(jnp.int32)
    far_given = quarter(1, 1, zlo)
    far_partner = swapped(far_given, "depth", 0)
    far_kept = quarter(0, 1, far_given)
    far = compose(0, "halves", leads, far_kept, far_partner)
    chip_partner = [swapped(far[0], "depth", 1)]
    near_given = quarter(1, 0, far[0])
    near_partner = swapped(near_given, "depth", 0)
    token, behind = lax.optimization_barrier((chip_partner[0], far[1]))
    chip_partner.append(swapped(behind, "depth", 1))
    near_kept = quarter(0, 0, token)
    images, base = [near_kept, near_partner, chip_partner], 0
    own = width // LANES // count
    if high > 1:
        current = compose(0, "plain", leads, *images)[0]
        order = [reverse_bits(place, rounds - 2) for place in range(high)]
        current = jnp.concatenate([current[:, p * own : (p + 1) * own] for p in order], axis=1)
        for level in range(2, rounds):
            half = current.shape[1] // 2
            kept = lax.dynamic_slice_in_dim(current, bits[level] * half, half, 1)
            given = lax.dynamic_slice_in_dim(current, (1 - bits[level]) * half, half, 1)
            partner = swapped(given, "depth", level)
            images, base = [kept, partner], level
            if level < rounds - 1:
                current = compose(level, "plain", leads, kept, partner)[0]
    core, last, first = compose(base, "borders", leads, *images)
    up, down = shifts("depth")
    halo = lax.ppermute(last, "depth", up) + lax.ppermute(first, "depth", down)
    inner = shade(True, core, halo)
    up, down = shifts("tile")

    def band(start):
        rows_at = slice(start, start + SUB)
        image = core[:, :, rows_at].reshape(8 * own, SUB, LANES)
        return jnp.concatenate([image, halo[None, rows_at]], axis=0)

    top = lax.ppermute(band(rows - SUB), "tile", up)
    bottom = lax.ppermute(band(0), "tile", down)
    return shade(False, core, halo, top, bottom, inner)


def solution(mesh):
    in_specs = (P("depth", "tile", None), P("tile"), P())
    out_specs = P(None, "tile", "depth")
    return jax.shard_map(
        per_device, mesh=mesh, in_specs=in_specs, out_specs=out_specs, check_vma=False
    )
```

```python
import functools
import math

import jax
import jax.numpy as jnp
from jax import lax
from jax.experimental import pallas as pl
from jax.experimental.pallas import tpu as pltpu
from jax.sharding import PartitionSpec as P

RADIUS = 8
LANES = 128
SUB = 8
LOG2E = math.log2(math.e)
OPACITY = 0.008
LIGHT = (0.48, 0.6, 0.64)
SPATIAL = 1.0 / 72.0
DEPTH_W = 20.0
NORMAL_W = 2.0
CENTRE = 127.5
AHEAD = 8


def shifts(axis):
    count = lax.axis_size(axis)
    up = [(i, i + 1) for i in range(count - 1)]
    return up, [(j, i) for i, j in up]


def swapped(block, axis, stride):
    count = lax.axis_size(axis)
    route = []
    for low in range(count):
        high = low | 1 << stride
        if high != low and high < count:
            route += [(low, high), (high, low)]
    return lax.ppermute(block, axis, route)


def edges_kernel(density_ref, zlo_ref, zhi_ref, ylo_ref, yhi_ref, planes, bands, lines, sems):
    cells, rows, width = density_ref.shape
    tiles = width // LANES
    copies = []
    for side in range(2):
        copies.append(
            pltpu.make_async_copy(
                density_ref.at[side * (cells - 1)], planes.at[side], sems.at[2 * side]
            )
        )
        copies.append(
            pltpu.make_async_copy(
                density_ref.at[:, side * (rows - SUB) : side * (rows - SUB) + SUB, :],
                bands.at[side],
                sems.at[2 * side + 1],
            )
        )
    for copy in copies:
        copy.start()
    for copy in copies:
        copy.wait()
    zlo_ref[...] = planes[0].astype(jnp.float32).astype(jnp.bfloat16)
    zhi_ref[...] = planes[1].astype(jnp.float32).astype(jnp.bfloat16)
    for side, ref in ((0, ylo_ref), (1, yhi_ref)):
        row = side * (SUB - 1)
        for z in range(cells):
            lines[z : z + 1, :] = bands[side, z, row : row + 1, :].astype(jnp.float32)
        ref[...] = lines[...].astype(jnp.bfloat16)


def edges(density):
    cells, rows, width = density.shape
    vmem = pl.BlockSpec(memory_space=pltpu.VMEM)
    plane = jax.ShapeDtypeStruct((rows, width), jnp.bfloat16)
    line = jax.ShapeDtypeStruct((cells, width), jnp.bfloat16)
    return pl.pallas_call(
        edges_kernel,
        out_shape=(plane, plane, line, line),
        in_specs=[pl.BlockSpec(memory_space=pl.ANY)],
        out_specs=[vmem] * 4,
        scratch_shapes=[
            pltpu.VMEM((2, rows, width), jnp.int32),
            pltpu.VMEM((2, cells, SUB, width), jnp.int32),
            pltpu.VMEM((cells, width), jnp.float32),
            pltpu.SemaphoreType.DMA((4,)),
        ],
        compiler_params=pltpu.CompilerParams(vmem_limit_bytes=52 << 20),
        name="edges",
    )(density)


def first_tile(place, own):
    position = lax.axis_index("depth")
    core, chip = position % 2, position // 2 % 2
    block = lax.rem(core + place[0], 2) + 2 * lax.rem(chip + place[1], 2) + 4 * place[2]
    return block * own


def pack_kernel(places, own, density_ref, *refs):
    fields, (stage, sems) = refs[:-2], refs[-2:]
    cells, rows, width = density_ref.shape
    tiles = width // LANES
    at = pl.ds(SUB, rows)

    def copy(z):
        return pltpu.make_async_copy(density_ref.at[z], stage.at[z], sems.at[z])

    for z in range(cells):
        copy(z).start()
    firsts = [first_tile(place, own) for place in places]

    def one(z, carry):
        copy(z).wait()
        for first, field in zip(firsts, fields):
            for j in range(own + 2):
                tile = jnp.clip(first + j - 1, 0, tiles - 1)
                cols = pl.ds(pl.multiple_of(tile * LANES, LANES), LANES)
                field[z + 1, j, at, :] = stage[z, :, cols].astype(jnp.float32) - CENTRE
        return carry

    lax.fori_loop(0, cells, one, 0)
    outside = jnp.full((rows, LANES), -CENTRE, jnp.float32)
    for first, field in zip(firsts, fields):

        @pl.when(first == 0)
        def _():
            for z in range(cells):
                field[z + 1, 0, at, :] = outside

        @pl.when(first + own == tiles)
        def _():
            for z in range(cells):
                field[z + 1, own + 1, at, :] = outside


def pack(density, places, count):
    cells, rows, width = density.shape
    own = width // LANES // count
    shape = jax.ShapeDtypeStruct((cells + 2, own + 2, rows + 2 * SUB, LANES), jnp.float32)
    return pl.pallas_call(
        functools.partial(pack_kernel, places, own),
        out_shape=[shape] * len(places),
        in_specs=[pl.BlockSpec(memory_space=pl.ANY)],
        out_specs=[pl.BlockSpec(memory_space=pltpu.VMEM)] * len(places),
        scratch_shapes=[
            pltpu.VMEM((cells, rows, width), jnp.int32),
            pltpu.SemaphoreType.DMA((cells,)),
        ],
        compiler_params=pltpu.CompilerParams(vmem_limit_bytes=12 << 20),
        cost_estimate=pl.CostEstimate(
            flops=2 * density.size, transcendentals=0, bytes_accessed=4 * density.size
        ),
        name="pack",
    )(density)


def integrate_kernel(
    place, flip_ref, coeff_ref, packed_ref, zlo_ref, zhi_ref, ylo_ref, yhi_ref, token_ref,
    out_ref, field_ref
):
    planes, wide, high, _ = field_ref.shape
    cells, own, rows = planes - 2, wide - 2, high - 2 * SUB
    count = lax.axis_size("depth")
    blocks = rows // SUB
    position = lax.axis_index("depth")
    first = first_tile(place, own)
    for j in range(own):
        cols = pl.ds(pl.multiple_of((first + j) * LANES, LANES), LANES)
        for ref, z in ((zlo_ref, 0), (zhi_ref, cells + 1)):
            field_ref[z, j + 1, SUB : SUB + rows, :] = ref[:, cols].astype(jnp.float32) - CENTRE
        for ref, y in ((ylo_ref, SUB - 1), (yhi_ref, SUB + rows)):
            lines = ref[:, cols].astype(jnp.float32) - CENTRE
            for z in range(cells):
                field_ref[z + 1, j + 1, y : y + 1, :] = lines[z : z + 1]
    flip = flip_ref[0]
    coeffs = []
    for row in range(4):
        scale = LOG2E if row == 0 else -LOG2E
        coeffs.append([coeff_ref[row, k] * (scale / CENTRE**k) for k in range(4)])
    sign = jnp.where(flip == 1, 1.0, -1.0)
    rate = sign * OPACITY
    lx, ly, lz = (0.65 * v for v in LIGHT)
    lane = lax.broadcasted_iota(jnp.int32, (SUB, LANES), 1)
    first_lane = lane == 0
    last_lane = lane == LANES - 1
    base = (position * cells).astype(jnp.float32)
    step = 1.0 / (cells * count)
    start = (base + 0.5) * step
    finish = (base + (cells - 0.5)) * step
    h_first = jnp.where(flip == 1, 1.0 - start, start)
    h_last = jnp.where(flip == 1, 1.0 - finish, finish)
    delta = jnp.where(flip == 1, -step, step)

    def poly(c, t):
        return c[0] + t * (c[1] + t * (c[2] + t * c[3]))

    def block(index, carry):
        out_j = index // blocks
        j = out_j + 1
        r = pl.multiple_of(index % blocks * SUB, SUB)
        at = pl.ds(r + SUB, SUB)
        zero = jnp.zeros((SUB, LANES), jnp.float32)
        tau = zero
        factor = jnp.ones((SUB, LANES), jnp.float32)
        between = zero
        sums = [zero] * 6
        below = field_ref[0, j, at, :]
        here = field_ref[1, j, at, :]
        for z in range(1, cells + 1):
            above = field_ref[z + 1, j, at, :]
            left = pltpu.roll(jnp.where(last_lane, field_ref[z, j - 1, at, :], here), 1, 1)
            right = jnp.where(first_lane, field_ref[z, j + 1, at, :], here)
            gx = pltpu.roll(right, LANES - 1, 1) - left
            gy = field_ref[z, j, pl.ds(r + SUB + 1, SUB), :]
            gy = gy - field_ref[z, j, pl.ds(r + SUB - 1, SUB), :]
            gz = above - below
            norm = lax.rsqrt(gx * gx + gy * gy + (gz * gz + 255.0 * 255.0))
            shade = 0.35 + jnp.abs((lx * gx + ly * gy + lz * gz) * norm)
            tau = tau + jnp.log2(1.0 + jnp.exp2(poly(coeffs[0], here)))
            following = jnp.exp2(rate * tau)
            weight = following - factor
            factor = following
            if z < cells:
                between = between + following
            tilt = weight * norm
            lit = weight * shade
            terms = [lit * (1.0 / (1.0 + jnp.exp2(poly(coeffs[k], here)))) for k in (1, 2, 3)]
            terms += [tilt * gx, tilt * gy, tilt * gz]
            sums = [s + t for s, t in zip(sums, terms)]
            below, here = here, above
        inverse = 1.0 / factor
        flipped = flip == 1
        scale = jnp.where(flipped, inverse, -1.0)
        out = pl.ds(r, SUB)
        for k in range(3):
            out_ref[k, out_j, out, :] = sums[k] * scale
            out_ref[k + 5, out_j, out, :] = sums[k + 3] * scale
        out_ref[3, out_j, out, :] = 1.0 - jnp.where(flipped, inverse, factor)
        out_ref[4, out_j, out, :] = (h_last * factor - h_first - delta * between) * scale
        return carry

    lax.fori_loop(0, own * blocks, block, 0)


def integrate(place, view_flip, tf_coeff, field, halos, token):
    planes, wide, high, _ = field.shape
    cells, own, rows = planes - 2, wide - 2, high - 2 * SUB
    smem = pl.BlockSpec(memory_space=pltpu.SMEM)
    vmem = pl.BlockSpec(memory_space=pltpu.VMEM)
    voxels = cells * rows * own * LANES
    return pl.pallas_call(
        functools.partial(integrate_kernel, place),
        out_shape=(
            jax.ShapeDtypeStruct((8, own, rows, LANES), jnp.float32),
            jax.ShapeDtypeStruct(field.shape, field.dtype),
        ),
        in_specs=[smem, smem, vmem, vmem, vmem, vmem, vmem, pl.BlockSpec(memory_space=pl.ANY)],
        out_specs=[vmem, vmem],
        input_output_aliases={2: 1},
        compiler_params=pltpu.CompilerParams(vmem_limit_bytes=8 << 20),
        cost_estimate=pl.CostEstimate(
            flops=70 * voxels, transcendentals=0, bytes_accessed=8 * voxels
        ),
        name="integrate",
    )(view_flip, tf_coeff, field, *halos, token)[0]


def shade_kernel(inner, core_ref, halo_ref, *rest):
    if inner:
        out_ref, planes, feats, buf_a, buf_b, acc = rest
    else:
        top_ref, bottom_ref, done_ref, out_ref, planes, feats, buf_a, buf_b, acc = rest
    _, tiles, rows, _ = core_ref.shape
    blocks = rows // SUB
    chosen = list(range(1, blocks - 1)) if inner else [0, blocks - 1]
    needed = sorted({n for b in chosen for n in (b - 1, b, b + 1)})

    def at(n):
        return pl.ds(SUB + n * SUB, SUB)

    for k in range(8):
        for n in needed:
            for t in (0, tiles + 1):
                planes[k, t, at(n), :] = jnp.zeros((SUB, LANES), jnp.float32)
            if 0 <= n < blocks:
                here = slice(n * SUB, n * SUB + SUB)
                side = halo_ref[here, :]
                for j in range(tiles):
                    planes[k, j + 1, at(n), :] = core_ref[k, j, here, :]
            else:
                ref = top_ref if n < 0 else bottom_ref
                side = ref[8 * tiles]
                for j in range(tiles):
                    planes[k, j + 1, at(n), :] = ref[k * tiles + j]
            left = side[:, RADIUS * k : RADIUS * k + RADIUS]
            right = side[:, RADIUS * (8 + k) : RADIUS * (9 + k)]
            planes[k, 0, at(n), LANES - RADIUS : LANES] = left
            planes[k, tiles + 1, at(n), 0:RADIUS] = right

    def features(t, carry):
        for n in needed:
            red, green, blue, alpha, depth, nx, ny, nz = [planes[k, t, at(n), :] for k in range(8)]
            facing = jnp.maximum(LIGHT[0] * nx + LIGHT[1] * ny + LIGHT[2] * nz, 0.0)
            lit = 0.4 + 0.6 * facing
            level = (DEPTH_W * LOG2E) * depth * depth
            level = level + (NORMAL_W * LOG2E) * (nx * nx + ny * ny + nz * nz)
            feats[0, t, at(n), :] = jnp.log2(jnp.maximum(alpha, 1e-37)) - level
            feats[1, t, at(n), :] = depth
            feats[2, t, at(n), :] = nx
            feats[3, t, at(n), :] = ny
            feats[4, t, at(n), :] = nz
            feats[5, t, at(n), :] = red * lit
            feats[6, t, at(n), :] = green * lit
            feats[7, t, at(n), :] = blue * lit
        return carry

    lax.fori_loop(0, tiles + 2, features, 0)
    lane = lax.broadcasted_iota(jnp.int32, (SUB, LANES), 1)

    def shift_setup(index):
        offset = index - RADIUS
        run = offset.astype(jnp.float32)
        spread = -(SPATIAL * LOG2E) * run * run
        border = jnp.where(offset < 0, LANES + offset, offset)
        amount = jnp.where(offset > 0, LANES - offset, -offset)
        below = lane < border
        take_other = (below & (offset >= 0)) | (jnp.logical_not(below) & (offset < 0))
        return jnp.where(offset < 0, 0, 2), amount, take_other, spread

    def moved(setup, k, j, n):
        other, amount, take_other, spread = setup
        mixed = jnp.where(take_other, feats[k, j + other, at(n), :], feats[k, j + 1, at(n), :])
        result = pltpu.roll(mixed, amount, 1)
        return result + spread if k == 0 else result

    def first_shift(k, carry):
        other, amount, take_other, spread = shift_setup(jnp.int32(0))
        for j in range(tiles):
            for n in needed:
                mixed = jnp.where(take_other, feats[k, j + other, at(n), :], feats[k, j + 1, at(n), :])
                result = pltpu.roll(mixed, amount, 1)
                buf_a[k, j, at(n), :] = result + jnp.where(k == 0, spread, 0.0)
        return carry

    lax.fori_loop(0, 8, first_shift, 0)
    for k in range(4):
        for j in range(tiles):
            for b in chosen:
                acc[k, j, at(b), :] = jnp.zeros((SUB, LANES), jnp.float32)

    offsets = sorted({o for b in chosen for o in range(SUB * b - RADIUS, SUB * b + RADIUS + 1)})

    def taps(buf, next_index, next_buf):
        pending, items = [], []
        if next_buf is not None:
            setup = shift_setup(next_index)
            items = [(k, j, n) for j in range(tiles) for n in needed for k in range(8)]
        pace = -(-len(items) // (len(offsets) * tiles))

        def pump(last=False):
            for _ in range(pace):
                if items:
                    pending.append((moved(setup, *items[0]),) + items.pop(0))
            while len(pending) > (0 if last else AHEAD):
                value, k, j, n = pending.pop(0)
                next_buf[k, j, at(n), :] = value

        for j in range(tiles):
            own, sums = {}, {}
            for o in offsets:
                pump()
                q = [buf[k, j, pl.ds(SUB + o, SUB), :] for k in range(8)]
                for b in chosen:
                    dy = o - SUB * b
                    if abs(dy) > RADIUS:
                        continue
                    if dy == -RADIUS:
                        own[b] = [feats[1, j + 1, at(b), :] * (2.0 * DEPTH_W * LOG2E)]
                        own[b] += [
                            feats[k, j + 1, at(b), :] * (2.0 * NORMAL_W * LOG2E) for k in (2, 3, 4)
                        ]
                        sums[b] = [acc[k, j, at(b), :] for k in range(4)]
                    p, s = own[b], sums[b]
                    power = (q[0] + p[0] * q[1]) + (p[1] * q[2] + p[2] * q[3])
                    power = power + (p[3] * q[4] - SPATIAL * LOG2E * dy * dy)
                    weight = jnp.exp2(power)
                    sums[b] = [s[k] + weight * q[5 + k] for k in range(3)] + [s[3] + weight]
                    if dy == RADIUS:
                        for k in range(4):
                            acc[k, j, at(b), :] = sums[b][k]
        while items or pending:
            pump(not items)

    def pair(step, carry):
        taps(buf_a, 2 * step + 1, buf_b)
        taps(buf_b, 2 * step + 2, buf_a)
        return carry

    lax.fori_loop(0, RADIUS, pair, 0)
    taps(buf_a, None, None)

    if not inner:
        for k in range(3):
            out_ref[k, SUB : rows - SUB, :] = done_ref[k, SUB : rows - SUB, :]
    for j in range(tiles):
        for b in chosen:
            depth, nx, ny, nz = [feats[k, j + 1, at(b), :] for k in (1, 2, 3, 4)]
            own = (DEPTH_W * LOG2E) * depth * depth
            own = own + (NORMAL_W * LOG2E) * (nx * nx + ny * ny + nz * nz)
            level = jnp.exp2(-own)
            scale = level / (1.0 + level * acc[3, j, at(b), :])
            for k in range(3):
                out_ref[k, b * SUB : b * SUB + SUB, j * LANES : (j + 1) * LANES] = (
                    acc[k, j, at(b), :] * scale
                )


def shade(inner, core, *rest):
    _, tiles, rows, _ = core.shape
    vmem = pl.BlockSpec(memory_space=pltpu.VMEM)
    wide = (8, tiles + 2, rows + 2 * SUB, LANES)
    moved = (8, tiles, rows + 2 * SUB, LANES)
    part = rows - 2 * SUB if inner else 2 * SUB
    work = part * tiles * LANES * (2 * RADIUS + 1) ** 2
    return pl.pallas_call(
        functools.partial(shade_kernel, inner),
        out_shape=jax.ShapeDtypeStruct((3, rows, tiles * LANES), jnp.float32),
        in_specs=[vmem] * (1 + len(rest)),
        out_specs=vmem,
        scratch_shapes=[
            pltpu.VMEM(wide, jnp.float32),
            pltpu.VMEM(wide, jnp.float32),
            pltpu.VMEM(moved, jnp.float32),
            pltpu.VMEM(moved, jnp.float32),
            pltpu.VMEM((4, tiles, rows + 2 * SUB, LANES), jnp.float32),
        ],
        compiler_params=pltpu.CompilerParams(vmem_limit_bytes=24 << 20),
        cost_estimate=pl.CostEstimate(
            flops=16 * work, transcendentals=work, bytes_accessed=8 * rows * tiles * LANES * 4
        ),
        name="shade_inner" if inner else "shade_outer",
    )(core, *rest)


def compose_kernel(base, pieces, mode, leads_ref, *refs):
    images, at_ref = [], 0
    for n in pieces:
        images.append(refs[at_ref : at_ref + n])
        at_ref += n
    outs = refs[at_ref:]
    _, tiles, rows, _ = outs[0].shape
    halves = outs if mode == "halves" else outs[:1]

    def plane(parts, k):
        size = 8 // len(parts)
        return parts[k // size], k % size

    def one(t, carry):
        j = t // (rows // SUB)
        at = pl.ds(pl.multiple_of(t % (rows // SUB) * SUB, SUB), SUB)

        def read(parts):
            found = [plane(parts, k) for k in range(8)]
            return [ref[k, j, at, :] for ref, k in found]

        current = read(images[0])
        for level, parts in enumerate(images[1:]):
            other = read(parts)
            leads = leads_ref[base + level] == 1
            share = jnp.where(leads, 1.0, 1.0 - other[3])
            other_share = jnp.where(leads, 1.0 - current[3], 1.0)
            current = [c * share + o * other_share for c, o in zip(current, other)]
        for k in range(8):
            ref, kk = plane(halves, k)
            ref[kk, j, at, :] = current[k]
        return carry

    lax.fori_loop(0, tiles * (rows // SUB), one, 0)
    if mode == "borders":
        out_ref, last_ref, first_ref = outs
        last_ref[...] = jnp.zeros((rows, LANES), jnp.float32)
        first_ref[...] = jnp.zeros((rows, LANES), jnp.float32)
        for k in range(8):
            last_ref[:, RADIUS * k : RADIUS * k + RADIUS] = out_ref[
                k, tiles - 1, :, LANES - RADIUS : LANES
            ]
            first_ref[:, RADIUS * (8 + k) : RADIUS * (9 + k)] = out_ref[k, 0, :, 0:RADIUS]


def compose(base, mode, leads, *images):
    images = [i if isinstance(i, (tuple, list)) else (i,) for i in images]
    _, tiles, rows, _ = images[0][0].shape
    smem = pl.BlockSpec(memory_space=pltpu.SMEM)
    vmem = pl.BlockSpec(memory_space=pltpu.VMEM)
    whole = jax.ShapeDtypeStruct((8, tiles, rows, LANES), jnp.float32)
    half = jax.ShapeDtypeStruct((4, tiles, rows, LANES), jnp.float32)
    border = jax.ShapeDtypeStruct((rows, LANES), jnp.float32)
    outs = {"plain": (whole,), "halves": (half, half), "borders": (whole, border, border)}[mode]
    parts = [p for image in images for p in image]
    return pl.pallas_call(
        functools.partial(compose_kernel, base, [len(i) for i in images], mode),
        out_shape=outs,
        in_specs=[smem] + [vmem] * len(parts),
        out_specs=[vmem] * len(outs),
        compiler_params=pltpu.CompilerParams(vmem_limit_bytes=8 << 20),
        cost_estimate=pl.CostEstimate(
            flops=0, transcendentals=0, bytes_accessed=32 * tiles * rows * LANES
        ),
        name="compose",
    )(leads, *parts)


def reverse_bits(value, rounds):
    result = 0
    for level in range(rounds):
        result = result * 2 + (value >> level) % 2
    return result


def per_device(density, view_flip, tf_coeff):
    cells, rows, width = density.shape
    count = lax.axis_size("depth")
    position = lax.axis_index("depth")
    flipped = view_flip[0]
    rounds = count.bit_length() - 1
    high = count // 4
    first_plane, last_plane, first_line, last_line = edges(density)
    up, down = shifts("depth")
    zlo = lax.ppermute(last_plane, "depth", up)
    zhi = lax.ppermute(first_plane, "depth", down)
    up, down = shifts("tile")
    ylo = lax.ppermute(last_line, "tile", up)
    yhi = lax.ppermute(first_line, "tile", down)

    halos = (zlo, zhi, ylo, yhi)
    quarters = ((1, 1), (0, 1), (1, 0), (0, 0))
    places = [quarter + (h,) for quarter in quarters for h in range(high)]
    fields = dict(zip(places, pack(density, places, count)))

    def quarter(core_bit, chip_bit, token):
        parts = []
        for h in range(high):
            place = (core_bit, chip_bit, h)
            parts.append(integrate(place, view_flip, tf_coeff, fields[place], halos, token))
        return parts[0] if high == 1 else jnp.concatenate(parts, axis=1)

    bits = [position // 2**level % 2 for level in range(rounds)]
    leads = jnp.stack([bit == flipped for bit in bits]).astype(jnp.int32)
    far_given = quarter(1, 1, view_flip)
    far_partner = swapped(far_given, "depth", 0)
    far_kept = quarter(0, 1, far_given)
    far = compose(0, "halves", leads, far_kept, far_partner)
    chip_partner = [swapped(far[0], "depth", 1)]
    near_given = quarter(1, 0, far[0])
    near_partner = swapped(near_given, "depth", 0)
    token, behind = lax.optimization_barrier((chip_partner[0], far[1]))
    chip_partner.append(swapped(behind, "depth", 1))
    near_kept = quarter(0, 0, token)
    images, base = [near_kept, near_partner, chip_partner], 0
    own = width // LANES // count
    if high > 1:
        current = compose(0, "plain", leads, *images)[0]
        order = [reverse_bits(place, rounds - 2) for place in range(high)]
        current = jnp.concatenate([current[:, p * own : (p + 1) * own] for p in order], axis=1)
        for level in range(2, rounds):
            half = current.shape[1] // 2
            kept = lax.dynamic_slice_in_dim(current, bits[level] * half, half, 1)
            given = lax.dynamic_slice_in_dim(current, (1 - bits[level]) * half, half, 1)
            partner = swapped(given, "depth", level)
            images, base = [kept, partner], level
            if level < rounds - 1:
                current = compose(level, "plain", leads, kept, partner)[0]
    core, last, first = compose(base, "borders", leads, *images)
    up, down = shifts("depth")
    halo = lax.ppermute(last, "depth", up) + lax.ppermute(first, "depth", down)
    inner = shade(True, core, halo)
    up, down = shifts("tile")

    def band(start):
        rows_at = slice(start, start + SUB)
        image = core[:, :, rows_at].reshape(8 * own, SUB, LANES)
        return jnp.concatenate([image, halo[None, rows_at]], axis=0)

    top = lax.ppermute(band(rows - SUB), "tile", up)
    bottom = lax.ppermute(band(0), "tile", down)
    return shade(False, core, halo, top, bottom, inner)


def solution(mesh):
    in_specs = (P("depth", "tile", None), P("tile"), P())
    out_specs = P(None, "tile", "depth")
    return jax.shard_map(
        per_device, mesh=mesh, in_specs=in_specs, out_specs=out_specs, check_vma=False
    )
```

```python
import functools
import math

import jax
import jax.numpy as jnp
from jax import lax
from jax.experimental import pallas as pl
from jax.experimental.pallas import tpu as pltpu
from jax.sharding import PartitionSpec as P

RADIUS = 8
LANES = 128
SUB = 8
LOG2E = math.log2(math.e)
OPACITY = 0.008
LIGHT = (0.48, 0.6, 0.64)
SPATIAL = 1.0 / 72.0
DEPTH_W = 20.0
NORMAL_W = 2.0
CENTRE = 127.5
AHEAD = 4


def shifts(axis):
    count = lax.axis_size(axis)
    up = [(i, i + 1) for i in range(count - 1)]
    return up, [(j, i) for i, j in up]


def swapped(block, axis, stride):
    count = lax.axis_size(axis)
    route = []
    for low in range(count):
        high = low | 1 << stride
        if high != low and high < count:
            route += [(low, high), (high, low)]
    return lax.ppermute(block, axis, route)


def edges_kernel(density_ref, zlo_ref, zhi_ref, ylo_ref, yhi_ref, planes, bands, lines, sems):
    cells, rows, width = density_ref.shape
    tiles = width // LANES
    copies = []
    for side in range(2):
        copies.append(
            pltpu.make_async_copy(
                density_ref.at[side * (cells - 1)], planes.at[side], sems.at[2 * side]
            )
        )
        copies.append(
            pltpu.make_async_copy(
                density_ref.at[:, side * (rows - SUB) : side * (rows - SUB) + SUB, :],
                bands.at[side],
                sems.at[2 * side + 1],
            )
        )
    for copy in copies:
        copy.start()
    for copy in copies:
        copy.wait()
    zlo_ref[...] = planes[0].astype(jnp.float32).astype(jnp.bfloat16)
    zhi_ref[...] = planes[1].astype(jnp.float32).astype(jnp.bfloat16)
    for side, ref in ((0, ylo_ref), (1, yhi_ref)):
        row = side * (SUB - 1)
        for z in range(cells):
            lines[z : z + 1, :] = bands[side, z, row : row + 1, :].astype(jnp.float32)
        ref[...] = lines[...].astype(jnp.bfloat16)


def edges(density):
    cells, rows, width = density.shape
    vmem = pl.BlockSpec(memory_space=pltpu.VMEM)
    plane = jax.ShapeDtypeStruct((rows, width), jnp.bfloat16)
    line = jax.ShapeDtypeStruct((cells, width), jnp.bfloat16)
    return pl.pallas_call(
        edges_kernel,
        out_shape=(plane, plane, line, line),
        in_specs=[pl.BlockSpec(memory_space=pl.ANY)],
        out_specs=[vmem] * 4,
        scratch_shapes=[
            pltpu.VMEM((2, rows, width), jnp.int32),
            pltpu.VMEM((2, cells, SUB, width), jnp.int32),
            pltpu.VMEM((cells, width), jnp.float32),
            pltpu.SemaphoreType.DMA((4,)),
        ],
        compiler_params=pltpu.CompilerParams(vmem_limit_bytes=52 << 20),
        name="edges",
    )(density)


def integrate_kernel(
    place, own, flip_ref, coeff_ref, density_ref, zlo_ref, zhi_ref, ylo_ref, yhi_ref, token_ref,
    out_ref, field, zlo_f, zhi_f, sems,
):
    cells, rows, width = density_ref.shape
    tiles = width // LANES
    blocks = rows // SUB
    count = tiles // own
    position = lax.axis_index("depth")
    c, y = position % 2, position // 2 % 2
    first = (lax.rem(c + place[0], 2) + 2 * lax.rem(y + place[1], 2) + 4 * place[2]) * own
    sources = [jnp.maximum(first - 1, 0)]
    sources += [first + j for j in range(own)]
    sources += [jnp.minimum(first + own, tiles - 1)]

    def copy(b, j):
        start = pl.multiple_of(sources[j] * LANES, LANES)
        return pltpu.make_async_copy(
            density_ref.at[:, pl.ds(b * SUB, SUB), pl.ds(start, LANES)],
            field.at[:, j, pl.ds(SUB + b * SUB, SUB), :],
            sems.at[b, j],
        )

    for b in range(blocks):
        for j in range(own + 2):
            copy(b, j).start()
    flip = flip_ref[0]
    for j in range(own):
        cols = pl.ds(pl.multiple_of((first + j) * LANES, LANES), LANES)
        zlo_f[j] = zlo_ref[:, cols].astype(jnp.float32) - CENTRE
        zhi_f[j] = zhi_ref[:, cols].astype(jnp.float32) - CENTRE
        top = ylo_ref[:, cols].astype(jnp.float32).astype(jnp.int32)
        bottom = yhi_ref[:, cols].astype(jnp.float32).astype(jnp.int32)
        for z in range(cells):
            field[z, j + 1, SUB - 1 : SUB, :] = top[z : z + 1]
            field[z, j + 1, SUB + rows : SUB + rows + 1, :] = bottom[z : z + 1]

    coeffs = []
    for row in range(4):
        scale = LOG2E if row == 0 else -LOG2E
        coeffs.append([coeff_ref[row, k] * (scale / CENTRE**k) for k in range(4)])
    sign = jnp.where(flip == 1, 1.0, -1.0)
    rate = sign * OPACITY
    lx, ly = LIGHT[0] / LIGHT[2], LIGHT[1] / LIGHT[2]
    ambient = 0.35 / (0.65 * LIGHT[2])
    lane = lax.broadcasted_iota(jnp.int32, (SUB, LANES), 1)
    first_lane = lane == 0
    last_lane = lane == LANES - 1
    base = (position * cells).astype(jnp.float32)
    step = 1.0 / (cells * count)
    start = (base + 0.5) * step
    finish = (base + (cells - 0.5)) * step
    h_first = jnp.where(flip == 1, 1.0 - start, start)
    h_last = jnp.where(flip == 1, 1.0 - finish, finish)
    delta = jnp.where(flip == 1, -step, step)

    def poly(c, t):
        return c[0] + t * (c[1] + t * (c[2] + t * c[3]))

    def arrive(b):
        for j in range(own + 2):
            copy(b, j).wait()
        at = pl.ds(SUB + b * SUB, SUB)

        @pl.when(first == 0)
        def _():
            for z in range(cells):
                field[z, 0, at, :] = jnp.zeros((SUB, LANES), jnp.int32)

        @pl.when(first + own == tiles)
        def _():
            for z in range(cells):
                field[z, own + 1, at, :] = jnp.zeros((SUB, LANES), jnp.int32)

    arrive(0)

    def block(b, carry):
        @pl.when(b + 1 < blocks)
        def _():
            arrive(b + 1)

        r = pl.multiple_of(b * SUB, SUB)
        for j in range(1, own + 1):
            column(r, j)
        return carry

    def column(r, j):
        at = pl.ds(r + SUB, SUB)
        zero = jnp.zeros((SUB, LANES), jnp.float32)
        tau = zero
        factor = jnp.ones((SUB, LANES), jnp.float32)
        between = zero
        sums = [zero] * 6
        below = zlo_f[j - 1, pl.ds(r, SUB), :]
        raw = field[0, j, at, :]
        here = raw.astype(jnp.float32) - CENTRE
        for z in range(cells):
            if z + 1 < cells:
                raw_above = field[z + 1, j, at, :]
                above = raw_above.astype(jnp.float32) - CENTRE
            else:
                raw_above = raw
                above = zhi_f[j - 1, pl.ds(r, SUB), :]
            left = pltpu.roll(jnp.where(last_lane, field[z, j - 1, at, :], raw), 1, 1)
            right = pltpu.roll(jnp.where(first_lane, field[z, j + 1, at, :], raw), LANES - 1, 1)
            gx = (right - left).astype(jnp.float32)
            up = field[z, j, pl.ds(r + SUB + 1, SUB), :]
            gy = (up - field[z, j, pl.ds(r + SUB - 1, SUB), :]).astype(jnp.float32)
            gz = above - below
            norm = lax.rsqrt(gx * gx + gy * gy + (gz * gz + 255.0 * 255.0))
            shade = ambient + jnp.abs((lx * gx + ly * gy + gz) * norm)
            tau = tau + jnp.log2(1.0 + jnp.exp2(poly(coeffs[0], here)))
            following = jnp.exp2(rate * tau)
            weight = following - factor
            factor = following
            if z < cells - 1:
                between = between + following
            tilt = weight * norm
            lit = weight * shade
            terms = [lit * (1.0 / (1.0 + jnp.exp2(poly(coeffs[k], here)))) for k in (1, 2, 3)]
            terms += [tilt * gx, tilt * gy, tilt * gz]
            sums = [s + t for s, t in zip(sums, terms)]
            below, here, raw = here, above, raw_above
        inverse = 1.0 / factor
        flipped = flip == 1
        scale = jnp.where(flipped, inverse, -1.0)
        out = pl.ds(r, SUB)
        for k in range(3):
            out_ref[k, j - 1, out, :] = sums[k] * (scale * (0.65 * LIGHT[2]))
            out_ref[k + 5, j - 1, out, :] = sums[k + 3] * scale
        out_ref[3, j - 1, out, :] = 1.0 - jnp.where(flipped, inverse, factor)
        out_ref[4, j - 1, out, :] = (h_last * factor - h_first - delta * between) * scale

    lax.fori_loop(0, blocks, block, 0)


def integrate(place, count, view_flip, tf_coeff, density, zlo, zhi, ylo, yhi, token):
    cells, rows, width = density.shape
    own = width // LANES // count
    smem = pl.BlockSpec(memory_space=pltpu.SMEM)
    vmem = pl.BlockSpec(memory_space=pltpu.VMEM)
    anywhere = pl.BlockSpec(memory_space=pl.ANY)
    voxels = cells * rows * own * LANES
    return pl.pallas_call(
        functools.partial(integrate_kernel, place, own),
        out_shape=jax.ShapeDtypeStruct((8, own, rows, LANES), jnp.float32),
        in_specs=[smem, smem, anywhere, vmem, vmem, vmem, vmem, anywhere],
        out_specs=vmem,
        scratch_shapes=[
            pltpu.VMEM((cells, own + 2, rows + 2 * SUB, LANES), jnp.int32),
            pltpu.VMEM((own, rows, LANES), jnp.float32),
            pltpu.VMEM((own, rows, LANES), jnp.float32),
            pltpu.SemaphoreType.DMA((rows // SUB, own + 2)),
        ],
        compiler_params=pltpu.CompilerParams(vmem_limit_bytes=52 << 20),
        cost_estimate=pl.CostEstimate(
            flops=70 * voxels, transcendentals=0, bytes_accessed=8 * voxels
        ),
        name="integrate",
    )(view_flip, tf_coeff, density, zlo, zhi, ylo, yhi, token)


def shade_kernel(inner, core_ref, halo_ref, *rest):
    if inner:
        out_ref, planes, feats, buf_a, buf_b, acc = rest
    else:
        top_ref, bottom_ref, done_ref, out_ref, planes, feats, buf_a, buf_b, acc = rest
    _, tiles, rows, _ = core_ref.shape
    blocks = rows // SUB
    chosen = list(range(1, blocks - 1)) if inner else [0, blocks - 1]
    needed = sorted({n for b in chosen for n in (b - 1, b, b + 1)})

    def at(n):
        return pl.ds(SUB + n * SUB, SUB)

    for k in range(8):
        for n in needed:
            for t in (0, tiles + 1):
                planes[k, t, at(n), :] = jnp.zeros((SUB, LANES), jnp.float32)
            if 0 <= n < blocks:
                here = slice(n * SUB, n * SUB + SUB)
                side = halo_ref[here, :]
                for j in range(tiles):
                    planes[k, j + 1, at(n), :] = core_ref[k, j, here, :]
            else:
                ref = top_ref if n < 0 else bottom_ref
                side = ref[8 * tiles]
                for j in range(tiles):
                    planes[k, j + 1, at(n), :] = ref[k * tiles + j]
            left = side[:, RADIUS * k : RADIUS * k + RADIUS]
            right = side[:, RADIUS * (8 + k) : RADIUS * (9 + k)]
            planes[k, 0, at(n), LANES - RADIUS : LANES] = left
            planes[k, tiles + 1, at(n), 0:RADIUS] = right

    def features(t, carry):
        for n in needed:
            red, green, blue, alpha, depth, nx, ny, nz = [planes[k, t, at(n), :] for k in range(8)]
            facing = jnp.maximum(LIGHT[0] * nx + LIGHT[1] * ny + LIGHT[2] * nz, 0.0)
            lit = 0.4 + 0.6 * facing
            level = (DEPTH_W * LOG2E) * depth * depth
            level = level + (NORMAL_W * LOG2E) * (nx * nx + ny * ny + nz * nz)
            feats[0, t, at(n), :] = jnp.log2(jnp.maximum(alpha, 1e-37)) - level
            feats[1, t, at(n), :] = depth
            feats[2, t, at(n), :] = nx
            feats[3, t, at(n), :] = ny
            feats[4, t, at(n), :] = nz
            feats[5, t, at(n), :] = red * lit
            feats[6, t, at(n), :] = green * lit
            feats[7, t, at(n), :] = blue * lit
        return carry

    lax.fori_loop(0, tiles + 2, features, 0)
    lane = lax.broadcasted_iota(jnp.int32, (SUB, LANES), 1)

    def shift_setup(index):
        offset = index - RADIUS + (index >= RADIUS).astype(jnp.int32)
        run = offset.astype(jnp.float32)
        spread = -(SPATIAL * LOG2E) * run * run
        border = jnp.where(offset < 0, LANES + offset, offset)
        amount = jnp.where(offset > 0, LANES - offset, -offset)
        below = lane < border
        take_other = (below & (offset >= 0)) | (jnp.logical_not(below) & (offset < 0))
        return jnp.where(offset < 0, 0, 2), amount, take_other, spread

    def moved(setup, k, j, n):
        other, amount, take_other, spread = setup
        mixed = jnp.where(take_other, feats[k, j + other, at(n), :], feats[k, j + 1, at(n), :])
        result = pltpu.roll(mixed, amount, 1)
        return result + spread if k == 0 else result

    for k in range(4):
        for j in range(tiles):
            for b in chosen:
                acc[k, j, at(b), :] = jnp.zeros((SUB, LANES), jnp.float32)

    offsets = sorted({o for b in chosen for o in range(SUB * b - RADIUS, SUB * b + RADIUS + 1)})

    def taps(buf, side, next_index, next_buf):
        pending, items = [], []
        if next_buf is not None:
            setup = shift_setup(next_index)
            items = [(k, j, n) for j in range(tiles) for n in needed for k in range(8)]
        pace = -(-len(items) // (len(offsets) * tiles))

        def pump(last=False):
            for _ in range(pace):
                if items:
                    pending.append((moved(setup, *items[0]),) + items.pop(0))
            while len(pending) > (0 if last else AHEAD):
                value, k, j, n = pending.pop(0)
                next_buf[k, j, at(n), :] = value

        for j in range(tiles):
            own, sums = {}, {}
            for o in offsets:
                pump()
                q = [buf[k, j + side, pl.ds(SUB + o, SUB), :] for k in range(8)]
                for b in chosen:
                    dy = o - SUB * b
                    if abs(dy) > RADIUS:
                        continue
                    if dy == -RADIUS:
                        own[b] = [feats[1, j + 1, at(b), :] * (2.0 * DEPTH_W * LOG2E)]
                        own[b] += [
                            feats[k, j + 1, at(b), :] * (2.0 * NORMAL_W * LOG2E) for k in (2, 3, 4)
                        ]
                        sums[b] = [acc[k, j, at(b), :] for k in range(4)]
                    p, s = own[b], sums[b]
                    power = (q[0] + p[0] * q[1]) + (p[1] * q[2] + p[2] * q[3])
                    power = power + (p[3] * q[4] - SPATIAL * LOG2E * dy * dy)
                    weight = jnp.exp2(power)
                    sums[b] = [s[k] + weight * q[5 + k] for k in range(3)] + [s[3] + weight]
                    if dy == RADIUS:
                        for k in range(4):
                            acc[k, j, at(b), :] = sums[b][k]
        while items or pending:
            pump(not items)

    def pair(step, carry):
        taps(buf_a, 0, 2 * step + 1, buf_b)
        taps(buf_b, 0, jnp.minimum(2 * step + 2, 2 * RADIUS - 1), buf_a)
        return carry

    taps(feats, 1, jnp.int32(0), buf_a)
    lax.fori_loop(0, RADIUS, pair, 0)

    if not inner:
        for k in range(3):
            out_ref[k, SUB : rows - SUB, :] = done_ref[k, SUB : rows - SUB, :]
    for j in range(tiles):
        for b in chosen:
            depth, nx, ny, nz = [feats[k, j + 1, at(b), :] for k in (1, 2, 3, 4)]
            own = (DEPTH_W * LOG2E) * depth * depth
            own = own + (NORMAL_W * LOG2E) * (nx * nx + ny * ny + nz * nz)
            level = jnp.exp2(-own)
            scale = level / (1.0 + level * acc[3, j, at(b), :])
            for k in range(3):
                out_ref[k, b * SUB : b * SUB + SUB, j * LANES : (j + 1) * LANES] = (
                    acc[k, j, at(b), :] * scale
                )


def shade(inner, core, *rest):
    _, tiles, rows, _ = core.shape
    vmem = pl.BlockSpec(memory_space=pltpu.VMEM)
    wide = (8, tiles + 2, rows + 2 * SUB, LANES)
    moved = (8, tiles, rows + 2 * SUB, LANES)
    part = rows - 2 * SUB if inner else 2 * SUB
    work = part * tiles * LANES * (2 * RADIUS + 1) ** 2
    return pl.pallas_call(
        functools.partial(shade_kernel, inner),
        out_shape=jax.ShapeDtypeStruct((3, rows, tiles * LANES), jnp.float32),
        in_specs=[vmem] * (1 + len(rest)),
        out_specs=vmem,
        scratch_shapes=[
            pltpu.VMEM(wide, jnp.float32),
            pltpu.VMEM(wide, jnp.float32),
            pltpu.VMEM(moved, jnp.float32),
            pltpu.VMEM(moved, jnp.float32),
            pltpu.VMEM((4, tiles, rows + 2 * SUB, LANES), jnp.float32),
        ],
        compiler_params=pltpu.CompilerParams(vmem_limit_bytes=24 << 20),
        cost_estimate=pl.CostEstimate(
            flops=16 * work, transcendentals=work, bytes_accessed=8 * rows * tiles * LANES * 4
        ),
        name="shade_inner" if inner else "shade_outer",
    )(core, *rest)


def compose_kernel(base, pieces, mode, leads_ref, *refs):
    images, at_ref = [], 0
    for n in pieces:
        images.append(refs[at_ref : at_ref + n])
        at_ref += n
    outs = refs[at_ref:]
    _, tiles, rows, _ = outs[0].shape
    halves = outs if mode == "halves" else outs[:1]

    def plane(parts, k):
        size = 8 // len(parts)
        return parts[k // size], k % size

    def one(t, carry):
        j = t // (rows // SUB)
        at = pl.ds(pl.multiple_of(t % (rows // SUB) * SUB, SUB), SUB)

        def read(parts):
            found = [plane(parts, k) for k in range(8)]
            return [ref[k, j, at, :] for ref, k in found]

        current = read(images[0])
        for level, parts in enumerate(images[1:]):
            other = read(parts)
            leads = leads_ref[base + level] == 1
            share = jnp.where(leads, 1.0, 1.0 - other[3])
            other_share = jnp.where(leads, 1.0 - current[3], 1.0)
            current = [c * share + o * other_share for c, o in zip(current, other)]
        for k in range(8):
            ref, kk = plane(halves, k)
            ref[kk, j, at, :] = current[k]
        return carry

    lax.fori_loop(0, tiles * (rows // SUB), one, 0)
    if mode == "borders":
        out_ref, last_ref, first_ref = outs
        last_ref[...] = jnp.zeros((rows, LANES), jnp.float32)
        first_ref[...] = jnp.zeros((rows, LANES), jnp.float32)
        for k in range(8):
            last_ref[:, RADIUS * k : RADIUS * k + RADIUS] = out_ref[
                k, tiles - 1, :, LANES - RADIUS : LANES
            ]
            first_ref[:, RADIUS * (8 + k) : RADIUS * (9 + k)] = out_ref[k, 0, :, 0:RADIUS]


def compose(base, mode, leads, *images):
    images = [i if isinstance(i, (tuple, list)) else (i,) for i in images]
    _, tiles, rows, _ = images[0][0].shape
    smem = pl.BlockSpec(memory_space=pltpu.SMEM)
    vmem = pl.BlockSpec(memory_space=pltpu.VMEM)
    whole = jax.ShapeDtypeStruct((8, tiles, rows, LANES), jnp.float32)
    half = jax.ShapeDtypeStruct((4, tiles, rows, LANES), jnp.float32)
    border = jax.ShapeDtypeStruct((rows, LANES), jnp.float32)
    outs = {"plain": (whole,), "halves": (half, half), "borders": (whole, border, border)}[mode]
    parts = [p for image in images for p in image]
    return pl.pallas_call(
        functools.partial(compose_kernel, base, [len(i) for i in images], mode),
        out_shape=outs,
        in_specs=[smem] + [vmem] * len(parts),
        out_specs=[vmem] * len(outs),
        compiler_params=pltpu.CompilerParams(vmem_limit_bytes=8 << 20),
        cost_estimate=pl.CostEstimate(
            flops=0, transcendentals=0, bytes_accessed=32 * tiles * rows * LANES
        ),
        name="compose",
    )(leads, *parts)


def reverse_bits(value, rounds):
    result = 0
    for level in range(rounds):
        result = result * 2 + (value >> level) % 2
    return result


def per_device(density, view_flip, tf_coeff):
    cells, rows, width = density.shape
    count = lax.axis_size("depth")
    position = lax.axis_index("depth")
    flipped = view_flip[0]
    rounds = count.bit_length() - 1
    high = count // 4
    first_plane, last_plane, first_line, last_line = edges(density)
    up, down = shifts("depth")
    zlo = lax.ppermute(last_plane, "depth", up)
    zhi = lax.ppermute(first_plane, "depth", down)
    up, down = shifts("tile")
    ylo = lax.ppermute(last_line, "tile", up)
    yhi = lax.ppermute(first_line, "tile", down)

    def quarter(core_bit, chip_bit, token):
        parts = [
            integrate(
                (core_bit, chip_bit, h), count, view_flip, tf_coeff, density, zlo, zhi, ylo, yhi, token
            )
            for h in range(high)
        ]
        return parts[0] if high == 1 else jnp.concatenate(parts, axis=1)

    bits = [position // 2**level % 2 for level in range(rounds)]
    leads = jnp.stack([bit == flipped for bit in bits]).astype(jnp.int32)
    far_given = quarter(1, 1, zlo)
    far_partner = swapped(far_given, "depth", 0)
    far_kept = quarter(0, 1, far_given)
    far = compose(0, "halves", leads, far_kept, far_partner)
    chip_partner = [swapped(far[0], "depth", 1)]
    near_given = quarter(1, 0, far[0])
    near_partner = swapped(near_given, "depth", 0)
    token, behind = lax.optimization_barrier((chip_partner[0], far[1]))
    chip_partner.append(swapped(behind, "depth", 1))
    near_kept = quarter(0, 0, token)
    images, base = [near_kept, near_partner, chip_partner], 0
    own = width // LANES // count
    if high > 1:
        current = compose(0, "plain", leads, *images)[0]
        order = [reverse_bits(place, rounds - 2) for place in range(high)]
        current = jnp.concatenate([current[:, p * own : (p + 1) * own] for p in order], axis=1)
        for level in range(2, rounds):
            half = current.shape[1] // 2
            kept = lax.dynamic_slice_in_dim(current, bits[level] * half, half, 1)
            given = lax.dynamic_slice_in_dim(current, (1 - bits[level]) * half, half, 1)
            partner = swapped(given, "depth", level)
            images, base = [kept, partner], level
            if level < rounds - 1:
                current = compose(level, "plain", leads, kept, partner)[0]
    core, last, first = compose(base, "borders", leads, *images)
    up, down = shifts("depth")
    halo = lax.ppermute(last, "depth", up) + lax.ppermute(first, "depth", down)
    inner = shade(True, core, halo)
    up, down = shifts("tile")

    def band(start):
        rows_at = slice(start, start + SUB)
        image = core[:, :, rows_at].reshape(8 * own, SUB, LANES)
        return jnp.concatenate([image, halo[None, rows_at]], axis=0)

    top = lax.ppermute(band(rows - SUB), "tile", up)
    bottom = lax.ppermute(band(0), "tile", down)
    return shade(False, core, halo, top, bottom, inner)


def solution(mesh):
    in_specs = (P("depth", "tile", None), P("tile"), P())
    out_specs = P(None, "tile", "depth")
    return jax.shard_map(
        per_device, mesh=mesh, in_specs=in_specs, out_specs=out_specs, check_vma=False
    )
```

```python
import functools
import math

import jax
import jax.numpy as jnp
from jax import lax
from jax.experimental import pallas as pl
from jax.experimental.pallas import tpu as pltpu
from jax.sharding import PartitionSpec as P

RADIUS = 8
LANES = 128
SUB = 8
LOG2E = math.log2(math.e)
OPACITY = 0.008
LIGHT = (0.48, 0.6, 0.64)
SPATIAL = 1.0 / 72.0
DEPTH_W = 20.0
NORMAL_W = 2.0
CENTRE = 127.5
AHEAD = 4


def shifts(axis):
    count = lax.axis_size(axis)
    up = [(i, i + 1) for i in range(count - 1)]
    return up, [(j, i) for i, j in up]


def swapped(block, axis, stride):
    count = lax.axis_size(axis)
    route = []
    for low in range(count):
        high = low | 1 << stride
        if high != low and high < count:
            route += [(low, high), (high, low)]
    return lax.ppermute(block, axis, route)


def edges_kernel(density_ref, zlo_ref, zhi_ref, ylo_ref, yhi_ref, planes, bands, lines, sems):
    cells, rows, width = density_ref.shape
    tiles = width // LANES
    copies = []
    for side in range(2):
        copies.append(
            pltpu.make_async_copy(
                density_ref.at[side * (cells - 1)], planes.at[side], sems.at[2 * side]
            )
        )
        copies.append(
            pltpu.make_async_copy(
                density_ref.at[:, side * (rows - SUB) : side * (rows - SUB) + SUB, :],
                bands.at[side],
                sems.at[2 * side + 1],
            )
        )
    for copy in copies:
        copy.start()
    for copy in copies:
        copy.wait()
    zlo_ref[...] = planes[0].astype(jnp.float32).astype(jnp.bfloat16)
    zhi_ref[...] = planes[1].astype(jnp.float32).astype(jnp.bfloat16)
    for side, ref in ((0, ylo_ref), (1, yhi_ref)):
        row = side * (SUB - 1)
        for z in range(cells):
            lines[z : z + 1, :] = bands[side, z, row : row + 1, :].astype(jnp.float32)
        ref[...] = lines[...].astype(jnp.bfloat16)


def edges(density):
    cells, rows, width = density.shape
    vmem = pl.BlockSpec(memory_space=pltpu.VMEM)
    plane = jax.ShapeDtypeStruct((rows, width), jnp.bfloat16)
    line = jax.ShapeDtypeStruct((cells, width), jnp.bfloat16)
    return pl.pallas_call(
        edges_kernel,
        out_shape=(plane, plane, line, line),
        in_specs=[pl.BlockSpec(memory_space=pl.ANY)],
        out_specs=[vmem] * 4,
        scratch_shapes=[
            pltpu.VMEM((2, rows, width), jnp.int32),
            pltpu.VMEM((2, cells, SUB, width), jnp.int32),
            pltpu.VMEM((cells, width), jnp.float32),
            pltpu.SemaphoreType.DMA((4,)),
        ],
        compiler_params=pltpu.CompilerParams(vmem_limit_bytes=52 << 20),
        name="edges",
    )(density)


def first_tile(place, own):
    position = lax.axis_index("depth")
    c, y = position % 2, position // 2 % 2
    return (lax.rem(c + place[0], 2) + 2 * lax.rem(y + place[1], 2) + 4 * place[2]) * own


def tile_copies(place, own, density_ref, field, sems):
    cells, rows, width = density_ref.shape
    tiles = width // LANES
    first = first_tile(place, own)
    sources = [jnp.maximum(first - 1, 0)]
    sources += [first + j for j in range(own)]
    sources += [jnp.minimum(first + own, tiles - 1)]

    def copy(b, j):
        start = pl.multiple_of(sources[j] * LANES, LANES)
        return pltpu.make_async_copy(
            density_ref.at[:, pl.ds(b * SUB, SUB), pl.ds(start, LANES)],
            field.at[:, j, pl.ds(SUB + b * SUB, SUB), :],
            sems.at[b, j],
        )

    def begin(b):
        for j in range(own + 2):
            copy(b, j).start()

    def arrive(b):
        for j in range(own + 2):
            copy(b, j).wait()
        at = pl.ds(SUB + b * SUB, SUB)

        @pl.when(first == 0)
        def _():
            for z in range(cells):
                field[z, 0, at, :] = jnp.zeros((SUB, LANES), jnp.int32)

        @pl.when(first + own == tiles)
        def _():
            for z in range(cells):
                field[z, own + 1, at, :] = jnp.zeros((SUB, LANES), jnp.int32)

    return begin, arrive


def stage_kernel(place, own, density_ref, field_ref, sems):
    blocks = density_ref.shape[1] // SUB
    begin, arrive = tile_copies(place, own, density_ref, field_ref, sems)
    for b in range(blocks):
        begin(b)
    lax.fori_loop(0, blocks, lambda b, carry: arrive(b) or carry, 0)


def stage(place, count, density):
    cells, rows, width = density.shape
    own = width // LANES // count
    shape = (cells, own + 2, rows + 2 * SUB, LANES)
    return pl.pallas_call(
        functools.partial(stage_kernel, place, own),
        out_shape=jax.ShapeDtypeStruct(shape, jnp.int32),
        in_specs=[pl.BlockSpec(memory_space=pl.ANY)],
        out_specs=pl.BlockSpec(memory_space=pltpu.VMEM),
        scratch_shapes=[pltpu.SemaphoreType.DMA((rows // SUB, own + 2))],
        compiler_params=pltpu.CompilerParams(vmem_limit_bytes=48 << 20),
        cost_estimate=pl.CostEstimate(
            flops=0, transcendentals=0, bytes_accessed=8 * cells * rows * (own + 2) * LANES
        ),
        name="stage",
    )(density)


def integrate_kernel(
    place, own, staged, flip_ref, coeff_ref, density_ref, zlo_ref, zhi_ref, ylo_ref, yhi_ref,
    token_ref, out_ref, *scratch,
):
    if staged:
        field, (zlo_f, zhi_f, top_f, bottom_f) = token_ref, scratch
    else:
        field, zlo_f, zhi_f, sems = scratch
    _, width = zlo_ref.shape
    cells, rows = ylo_ref.shape[0], zlo_ref.shape[0]
    tiles = width // LANES
    blocks = rows // SUB
    count = tiles // own
    position = lax.axis_index("depth")
    first = first_tile(place, own)
    if not staged:
        begin, arrive = tile_copies(place, own, density_ref, field, sems)
        for b in range(blocks):
            begin(b)
    flip = flip_ref[0]
    for j in range(own):
        cols = pl.ds(pl.multiple_of((first + j) * LANES, LANES), LANES)
        zlo_f[j] = zlo_ref[:, cols].astype(jnp.float32) - CENTRE
        zhi_f[j] = zhi_ref[:, cols].astype(jnp.float32) - CENTRE
        top = ylo_ref[:, cols].astype(jnp.float32).astype(jnp.int32)
        bottom = yhi_ref[:, cols].astype(jnp.float32).astype(jnp.int32)
        if staged:
            top_f[j] = top
            bottom_f[j] = bottom
        for z in range(0 if staged else cells):
            field[z, j + 1, SUB - 1 : SUB, :] = top[z : z + 1]
            field[z, j + 1, SUB + rows : SUB + rows + 1, :] = bottom[z : z + 1]

    coeffs = []
    for row in range(4):
        scale = LOG2E if row == 0 else -LOG2E
        coeffs.append([coeff_ref[row, k] * (scale / CENTRE**k) for k in range(4)])
    sign = jnp.where(flip == 1, 1.0, -1.0)
    rate = sign * OPACITY
    lx, ly = LIGHT[0] / LIGHT[2], LIGHT[1] / LIGHT[2]
    ambient = 0.35 / (0.65 * LIGHT[2])
    lane = lax.broadcasted_iota(jnp.int32, (SUB, LANES), 1)
    first_lane = lane == 0
    last_lane = lane == LANES - 1
    base = (position * cells).astype(jnp.float32)
    step = 1.0 / (cells * count)
    start = (base + 0.5) * step
    finish = (base + (cells - 0.5)) * step
    h_first = jnp.where(flip == 1, 1.0 - start, start)
    h_last = jnp.where(flip == 1, 1.0 - finish, finish)
    delta = jnp.where(flip == 1, -step, step)

    def poly(c, t):
        return c[0] + t * (c[1] + t * (c[2] + t * c[3]))

    row = lax.broadcasted_iota(jnp.int32, (SUB, LANES), 0)
    if not staged:
        arrive(0)

    def block(b, carry):
        if not staged:

            @pl.when(b + 1 < blocks)
            def _():
                arrive(b + 1)

        r = pl.multiple_of(b * SUB, SUB)
        for j in range(1, own + 1):
            column(r, j)
        return carry

    def column(r, j):
        at = pl.ds(r + SUB, SUB)
        zero = jnp.zeros((SUB, LANES), jnp.float32)
        tau = zero
        factor = jnp.ones((SUB, LANES), jnp.float32)
        between = zero
        sums = [zero] * 6
        below = zlo_f[j - 1, pl.ds(r, SUB), :]
        raw = field[0, j, at, :]
        here = raw.astype(jnp.float32) - CENTRE
        for z in range(cells):
            if z + 1 < cells:
                raw_above = field[z + 1, j, at, :]
                above = raw_above.astype(jnp.float32) - CENTRE
            else:
                raw_above = raw
                above = zhi_f[j - 1, pl.ds(r, SUB), :]
            left = pltpu.roll(jnp.where(last_lane, field[z, j - 1, at, :], raw), 1, 1)
            right = pltpu.roll(jnp.where(first_lane, field[z, j + 1, at, :], raw), LANES - 1, 1)
            gx = (right - left).astype(jnp.float32)
            up = field[z, j, pl.ds(r + SUB + 1, SUB), :]
            down = field[z, j, pl.ds(r + SUB - 1, SUB), :]
            if staged:
                up = jnp.where(row + r == rows - 1, bottom_f[j - 1, z : z + 1, :], up)
                down = jnp.where(row + r == 0, top_f[j - 1, z : z + 1, :], down)
            gy = (up - down).astype(jnp.float32)
            gz = above - below
            norm = lax.rsqrt(gx * gx + gy * gy + (gz * gz + 255.0 * 255.0))
            shade = ambient + jnp.abs((lx * gx + ly * gy + gz) * norm)
            tau = tau + jnp.log2(1.0 + jnp.exp2(poly(coeffs[0], here)))
            following = jnp.exp2(rate * tau)
            weight = following - factor
            factor = following
            if z < cells - 1:
                between = between + following
            tilt = weight * norm
            lit = weight * shade
            terms = [lit * (1.0 / (1.0 + jnp.exp2(poly(coeffs[k], here)))) for k in (1, 2, 3)]
            terms += [tilt * gx, tilt * gy, tilt * gz]
            sums = [s + t for s, t in zip(sums, terms)]
            below, here, raw = here, above, raw_above
        inverse = 1.0 / factor
        flipped = flip == 1
        scale = jnp.where(flipped, inverse, -1.0)
        out = pl.ds(r, SUB)
        for k in range(3):
            out_ref[k, j - 1, out, :] = sums[k] * (scale * (0.65 * LIGHT[2]))
            out_ref[k + 5, j - 1, out, :] = sums[k + 3] * scale
        out_ref[3, j - 1, out, :] = 1.0 - jnp.where(flipped, inverse, factor)
        out_ref[4, j - 1, out, :] = (h_last * factor - h_first - delta * between) * scale

    lax.fori_loop(0, blocks, block, 0)


def integrate(place, count, view_flip, tf_coeff, density, zlo, zhi, ylo, yhi, token, staged):
    cells, rows, width = density.shape
    own = width // LANES // count
    smem = pl.BlockSpec(memory_space=pltpu.SMEM)
    vmem = pl.BlockSpec(memory_space=pltpu.VMEM)
    anywhere = pl.BlockSpec(memory_space=pl.ANY)
    voxels = cells * rows * own * LANES
    copied = pltpu.VMEM((cells, own + 2, rows + 2 * SUB, LANES), jnp.int32)
    borders = [pltpu.VMEM((own, rows, LANES), jnp.float32)] * 2
    line = pltpu.VMEM((own, cells, LANES), jnp.int32)
    sems = pltpu.SemaphoreType.DMA((rows // SUB, own + 2))
    return pl.pallas_call(
        functools.partial(integrate_kernel, place, own, staged),
        out_shape=jax.ShapeDtypeStruct((8, own, rows, LANES), jnp.float32),
        in_specs=[smem, smem, anywhere] + [vmem] * 4 + [vmem if staged else anywhere],
        out_specs=vmem,
        scratch_shapes=(borders + [line, line]) if staged else ([copied] + borders + [sems]),
        compiler_params=pltpu.CompilerParams(vmem_limit_bytes=(40 if staged else 52) << 20),
        cost_estimate=pl.CostEstimate(
            flops=70 * voxels, transcendentals=0, bytes_accessed=8 * voxels
        ),
        name="integrate",
    )(view_flip, tf_coeff, view_flip if staged else density, zlo, zhi, ylo, yhi, token)


def shade_kernel(inner, core_ref, halo_ref, *rest):
    if inner:
        out_ref, planes, feats, buf_a, buf_b, acc = rest
    else:
        top_ref, bottom_ref, done_ref, out_ref, planes, feats, buf_a, buf_b, acc = rest
    _, tiles, rows, _ = core_ref.shape
    blocks = rows // SUB
    chosen = list(range(1, blocks - 1)) if inner else [0, blocks - 1]
    needed = sorted({n for b in chosen for n in (b - 1, b, b + 1)})

    def at(n):
        return pl.ds(SUB + n * SUB, SUB)

    for k in range(8):
        for n in needed:
            for t in (0, tiles + 1):
                planes[k, t, at(n), :] = jnp.zeros((SUB, LANES), jnp.float32)
            if 0 <= n < blocks:
                here = slice(n * SUB, n * SUB + SUB)
                side = halo_ref[here, :]
                for j in range(tiles):
                    planes[k, j + 1, at(n), :] = core_ref[k, j, here, :]
            else:
                ref = top_ref if n < 0 else bottom_ref
                side = ref[8 * tiles]
                for j in range(tiles):
                    planes[k, j + 1, at(n), :] = ref[k * tiles + j]
            left = side[:, RADIUS * k : RADIUS * k + RADIUS]
            right = side[:, RADIUS * (8 + k) : RADIUS * (9 + k)]
            planes[k, 0, at(n), LANES - RADIUS : LANES] = left
            planes[k, tiles + 1, at(n), 0:RADIUS] = right

    def features(t, carry):
        for n in needed:
            red, green, blue, alpha, depth, nx, ny, nz = [planes[k, t, at(n), :] for k in range(8)]
            facing = jnp.maximum(LIGHT[0] * nx + LIGHT[1] * ny + LIGHT[2] * nz, 0.0)
            lit = 0.4 + 0.6 * facing
            level = (DEPTH_W * LOG2E) * depth * depth
            level = level + (NORMAL_W * LOG2E) * (nx * nx + ny * ny + nz * nz)
            feats[0, t, at(n), :] = jnp.log2(jnp.maximum(alpha, 1e-37)) - level
            feats[1, t, at(n), :] = depth
            feats[2, t, at(n), :] = nx
            feats[3, t, at(n), :] = ny
            feats[4, t, at(n), :] = nz
            feats[5, t, at(n), :] = red * lit
            feats[6, t, at(n), :] = green * lit
            feats[7, t, at(n), :] = blue * lit
        return carry

    lax.fori_loop(0, tiles + 2, features, 0)
    lane = lax.broadcasted_iota(jnp.int32, (SUB, LANES), 1)

    def shift_setup(index):
        offset = index - RADIUS + (index >= RADIUS).astype(jnp.int32)
        run = offset.astype(jnp.float32)
        spread = -(SPATIAL * LOG2E) * run * run
        border = jnp.where(offset < 0, LANES + offset, offset)
        amount = jnp.where(offset > 0, LANES - offset, -offset)
        below = lane < border
        take_other = (below & (offset >= 0)) | (jnp.logical_not(below) & (offset < 0))
        return jnp.where(offset < 0, 0, 2), amount, take_other, spread

    def moved(setup, k, j, n):
        other, amount, take_other, spread = setup
        mixed = jnp.where(take_other, feats[k, j + other, at(n), :], feats[k, j + 1, at(n), :])
        result = pltpu.roll(mixed, amount, 1)
        return result + spread if k == 0 else result

    for k in range(4):
        for j in range(tiles):
            for b in chosen:
                acc[k, j, at(b), :] = jnp.zeros((SUB, LANES), jnp.float32)

    offsets = sorted({o for b in chosen for o in range(SUB * b - RADIUS, SUB * b + RADIUS + 1)})

    def taps(buf, side, next_index, next_buf):
        pending, items = [], []
        if next_buf is not None:
            setup = shift_setup(next_index)
            items = [(k, j, n) for j in range(tiles) for n in needed for k in range(8)]
        pace = -(-len(items) // (len(offsets) * tiles))

        def pump(last=False):
            for _ in range(pace):
                if items:
                    pending.append((moved(setup, *items[0]),) + items.pop(0))
            while len(pending) > (0 if last else AHEAD):
                value, k, j, n = pending.pop(0)
                next_buf[k, j, at(n), :] = value

        for j in range(tiles):
            own, sums = {}, {}
            for o in offsets:
                pump()
                q = [buf[k, j + side, pl.ds(SUB + o, SUB), :] for k in range(8)]
                for b in chosen:
                    dy = o - SUB * b
                    if abs(dy) > RADIUS:
                        continue
                    if dy == -RADIUS:
                        own[b] = [feats[1, j + 1, at(b), :] * (2.0 * DEPTH_W * LOG2E)]
                        own[b] += [
                            feats[k, j + 1, at(b), :] * (2.0 * NORMAL_W * LOG2E) for k in (2, 3, 4)
                        ]
                        sums[b] = [acc[k, j, at(b), :] for k in range(4)]
                    p, s = own[b], sums[b]
                    power = (q[0] + p[0] * q[1]) + (p[1] * q[2] + p[2] * q[3])
                    power = power + (p[3] * q[4] - SPATIAL * LOG2E * dy * dy)
                    weight = jnp.exp2(power)
                    sums[b] = [s[k] + weight * q[5 + k] for k in range(3)] + [s[3] + weight]
                    if dy == RADIUS:
                        for k in range(4):
                            acc[k, j, at(b), :] = sums[b][k]
        while items or pending:
            pump(not items)

    def pair(step, carry):
        taps(buf_a, 0, 2 * step + 1, buf_b)
        taps(buf_b, 0, jnp.minimum(2 * step + 2, 2 * RADIUS - 1), buf_a)
        return carry

    taps(feats, 1, jnp.int32(0), buf_a)
    lax.fori_loop(0, RADIUS, pair, 0)

    if not inner:
        for k in range(3):
            out_ref[k, SUB : rows - SUB, :] = done_ref[k, SUB : rows - SUB, :]
    for j in range(tiles):
        for b in chosen:
            depth, nx, ny, nz = [feats[k, j + 1, at(b), :] for k in (1, 2, 3, 4)]
            own = (DEPTH_W * LOG2E) * depth * depth
            own = own + (NORMAL_W * LOG2E) * (nx * nx + ny * ny + nz * nz)
            level = jnp.exp2(-own)
            scale = level / (1.0 + level * acc[3, j, at(b), :])
            for k in range(3):
                out_ref[k, b * SUB : b * SUB + SUB, j * LANES : (j + 1) * LANES] = (
                    acc[k, j, at(b), :] * scale
                )


def shade(inner, core, *rest):
    _, tiles, rows, _ = core.shape
    vmem = pl.BlockSpec(memory_space=pltpu.VMEM)
    wide = (8, tiles + 2, rows + 2 * SUB, LANES)
    moved = (8, tiles, rows + 2 * SUB, LANES)
    part = rows - 2 * SUB if inner else 2 * SUB
    work = part * tiles * LANES * (2 * RADIUS + 1) ** 2
    return pl.pallas_call(
        functools.partial(shade_kernel, inner),
        out_shape=jax.ShapeDtypeStruct((3, rows, tiles * LANES), jnp.float32),
        in_specs=[vmem] * (1 + len(rest)),
        out_specs=vmem,
        scratch_shapes=[
            pltpu.VMEM(wide, jnp.float32),
            pltpu.VMEM(wide, jnp.float32),
            pltpu.VMEM(moved, jnp.float32),
            pltpu.VMEM(moved, jnp.float32),
            pltpu.VMEM((4, tiles, rows + 2 * SUB, LANES), jnp.float32),
        ],
        compiler_params=pltpu.CompilerParams(vmem_limit_bytes=24 << 20),
        cost_estimate=pl.CostEstimate(
            flops=16 * work, transcendentals=work, bytes_accessed=8 * rows * tiles * LANES * 4
        ),
        name="shade_inner" if inner else "shade_outer",
    )(core, *rest)


def compose_kernel(base, pieces, mode, leads_ref, *refs):
    images, at_ref = [], 0
    for n in pieces:
        images.append(refs[at_ref : at_ref + n])
        at_ref += n
    outs = refs[at_ref:]
    _, tiles, rows, _ = outs[0].shape
    halves = outs if mode == "halves" else outs[:1]

    def plane(parts, k):
        size = 8 // len(parts)
        return parts[k // size], k % size

    def one(t, carry):
        j = t // (rows // SUB)
        at = pl.ds(pl.multiple_of(t % (rows // SUB) * SUB, SUB), SUB)

        def read(parts):
            found = [plane(parts, k) for k in range(8)]
            return [ref[k, j, at, :] for ref, k in found]

        current = read(images[0])
        for level, parts in enumerate(images[1:]):
            other = read(parts)
            leads = leads_ref[base + level] == 1
            share = jnp.where(leads, 1.0, 1.0 - other[3])
            other_share = jnp.where(leads, 1.0 - current[3], 1.0)
            current = [c * share + o * other_share for c, o in zip(current, other)]
        for k in range(8):
            ref, kk = plane(halves, k)
            ref[kk, j, at, :] = current[k]
        return carry

    lax.fori_loop(0, tiles * (rows // SUB), one, 0)
    if mode == "borders":
        out_ref, last_ref, first_ref = outs
        last_ref[...] = jnp.zeros((rows, LANES), jnp.float32)
        first_ref[...] = jnp.zeros((rows, LANES), jnp.float32)
        for k in range(8):
            last_ref[:, RADIUS * k : RADIUS * k + RADIUS] = out_ref[
                k, tiles - 1, :, LANES - RADIUS : LANES
            ]
            first_ref[:, RADIUS * (8 + k) : RADIUS * (9 + k)] = out_ref[k, 0, :, 0:RADIUS]


def compose(base, mode, leads, *images):
    images = [i if isinstance(i, (tuple, list)) else (i,) for i in images]
    _, tiles, rows, _ = images[0][0].shape
    smem = pl.BlockSpec(memory_space=pltpu.SMEM)
    vmem = pl.BlockSpec(memory_space=pltpu.VMEM)
    whole = jax.ShapeDtypeStruct((8, tiles, rows, LANES), jnp.float32)
    half = jax.ShapeDtypeStruct((4, tiles, rows, LANES), jnp.float32)
    border = jax.ShapeDtypeStruct((rows, LANES), jnp.float32)
    outs = {"plain": (whole,), "halves": (half, half), "borders": (whole, border, border)}[mode]
    parts = [p for image in images for p in image]
    return pl.pallas_call(
        functools.partial(compose_kernel, base, [len(i) for i in images], mode),
        out_shape=outs,
        in_specs=[smem] + [vmem] * len(parts),
        out_specs=[vmem] * len(outs),
        compiler_params=pltpu.CompilerParams(vmem_limit_bytes=8 << 20),
        cost_estimate=pl.CostEstimate(
            flops=0, transcendentals=0, bytes_accessed=32 * tiles * rows * LANES
        ),
        name="compose",
    )(leads, *parts)


def reverse_bits(value, rounds):
    result = 0
    for level in range(rounds):
        result = result * 2 + (value >> level) % 2
    return result


def per_device(density, view_flip, tf_coeff):
    cells, rows, width = density.shape
    count = lax.axis_size("depth")
    position = lax.axis_index("depth")
    flipped = view_flip[0]
    rounds = count.bit_length() - 1
    high = count // 4
    first_plane, last_plane, first_line, last_line = edges(density)
    up, down = shifts("depth")
    zlo = lax.ppermute(last_plane, "depth", up)
    zhi = lax.ppermute(first_plane, "depth", down)
    up, down = shifts("tile")
    ylo = lax.ppermute(last_line, "tile", up)
    yhi = lax.ppermute(first_line, "tile", down)

    def quarter(core_bit, chip_bit, token):
        parts = []
        for h in range(high):
            place = (core_bit, chip_bit, h)
            given = stage(place, count, density) if token is None else token
            parts.append(
                integrate(
                    place, count, view_flip, tf_coeff, density, zlo, zhi, ylo, yhi, given,
                    token is None,
                )
            )
        return parts[0] if high == 1 else jnp.concatenate(parts, axis=1)

    bits = [position // 2**level % 2 for level in range(rounds)]
    leads = jnp.stack([bit == flipped for bit in bits]).astype(jnp.int32)
    far_given = quarter(1, 1, None)
    far_partner = swapped(far_given, "depth", 0)
    far_kept = quarter(0, 1, far_given)
    far = compose(0, "halves", leads, far_kept, far_partner)
    chip_partner = [swapped(far[0], "depth", 1)]
    near_given = quarter(1, 0, far[0])
    near_partner = swapped(near_given, "depth", 0)
    token, behind = lax.optimization_barrier((chip_partner[0], far[1]))
    chip_partner.append(swapped(behind, "depth", 1))
    near_kept = quarter(0, 0, token)
    images, base = [near_kept, near_partner, chip_partner], 0
    own = width // LANES // count
    if high > 1:
        current = compose(0, "plain", leads, *images)[0]
        order = [reverse_bits(place, rounds - 2) for place in range(high)]
        current = jnp.concatenate([current[:, p * own : (p + 1) * own] for p in order], axis=1)
        for level in range(2, rounds):
            half = current.shape[1] // 2
            kept = lax.dynamic_slice_in_dim(current, bits[level] * half, half, 1)
            given = lax.dynamic_slice_in_dim(current, (1 - bits[level]) * half, half, 1)
            partner = swapped(given, "depth", level)
            images, base = [kept, partner], level
            if level < rounds - 1:
                current = compose(level, "plain", leads, kept, partner)[0]
    core, last, first = compose(base, "borders", leads, *images)
    up, down = shifts("depth")
    halo = lax.ppermute(last, "depth", up) + lax.ppermute(first, "depth", down)
    inner = shade(True, core, halo)
    up, down = shifts("tile")

    def band(start):
        rows_at = slice(start, start + SUB)
        image = core[:, :, rows_at].reshape(8 * own, SUB, LANES)
        return jnp.concatenate([image, halo[None, rows_at]], axis=0)

    top = lax.ppermute(band(rows - SUB), "tile", up)
    bottom = lax.ppermute(band(0), "tile", down)
    return shade(False, core, halo, top, bottom, inner)


def solution(mesh):
    in_specs = (P("depth", "tile", None), P("tile"), P())
    out_specs = P(None, "tile", "depth")
    return jax.shard_map(
        per_device, mesh=mesh, in_specs=in_specs, out_specs=out_specs, check_vma=False
    )
```

```python
import functools
import math

import jax
import jax.numpy as jnp
from jax import lax
from jax.experimental import pallas as pl
from jax.experimental.pallas import tpu as pltpu
from jax.sharding import PartitionSpec as P

RADIUS = 8
LANES = 128
SUB = 8
LOG2E = math.log2(math.e)
OPACITY = 0.008
LIGHT = (0.48, 0.6, 0.64)
SPATIAL = 1.0 / 72.0
DEPTH_W = 20.0
NORMAL_W = 2.0
CENTRE = 127.5
AHEAD = 4


def shifts(axis):
    count = lax.axis_size(axis)
    up = [(i, i + 1) for i in range(count - 1)]
    return up, [(j, i) for i, j in up]


def swapped(block, axis, stride):
    count = lax.axis_size(axis)
    route = []
    for low in range(count):
        high = low | 1 << stride
        if high != low and high < count:
            route += [(low, high), (high, low)]
    return lax.ppermute(block, axis, route)


def edges_kernel(density_ref, zlo_ref, zhi_ref, ylo_ref, yhi_ref, planes, bands, lines, sems):
    cells, rows, width = density_ref.shape
    tiles = width // LANES
    copies = []
    for side in range(2):
        copies.append(
            pltpu.make_async_copy(
                density_ref.at[side * (cells - 1)], planes.at[side], sems.at[2 * side]
            )
        )
        copies.append(
            pltpu.make_async_copy(
                density_ref.at[:, side * (rows - 1) : side * (rows - 1) + 1, :],
                bands.at[side],
                sems.at[2 * side + 1],
            )
        )
    for copy in copies:
        copy.start()
    for copy in copies:
        copy.wait()
    zlo_ref[...] = planes[0].astype(jnp.float32).astype(jnp.bfloat16)
    zhi_ref[...] = planes[1].astype(jnp.float32).astype(jnp.bfloat16)
    for side, ref in ((0, ylo_ref), (1, yhi_ref)):
        for z in range(cells):
            lines[z : z + 1, :] = bands[side, z].astype(jnp.float32)
        ref[...] = lines[...].astype(jnp.bfloat16)


def edges(density):
    cells, rows, width = density.shape
    vmem = pl.BlockSpec(memory_space=pltpu.VMEM)
    plane = jax.ShapeDtypeStruct((rows, width), jnp.bfloat16)
    line = jax.ShapeDtypeStruct((cells, width), jnp.bfloat16)
    return pl.pallas_call(
        edges_kernel,
        out_shape=(plane, plane, line, line),
        in_specs=[pl.BlockSpec(memory_space=pl.ANY)],
        out_specs=[vmem] * 4,
        scratch_shapes=[
            pltpu.VMEM((2, rows, width), jnp.int32),
            pltpu.VMEM((2, cells, 1, width), jnp.int32),
            pltpu.VMEM((cells, width), jnp.float32),
            pltpu.SemaphoreType.DMA((4,)),
        ],
        compiler_params=pltpu.CompilerParams(vmem_limit_bytes=52 << 20),
        name="edges",
    )(density)


def first_tile(place, own):
    position = lax.axis_index("depth")
    c, y = position % 2, position // 2 % 2
    return (lax.rem(c + place[0], 2) + 2 * lax.rem(y + place[1], 2) + 4 * place[2]) * own


def tile_copies(place, own, density_ref, field, sems):
    cells, rows, width = density_ref.shape
    tiles = width // LANES
    first = first_tile(place, own)
    sources = [jnp.maximum(first - 1, 0)]
    sources += [first + j for j in range(own)]
    sources += [jnp.minimum(first + own, tiles - 1)]

    def copy(b, j):
        start = pl.multiple_of(sources[j] * LANES, LANES)
        return pltpu.make_async_copy(
            density_ref.at[:, pl.ds(b * SUB, SUB), pl.ds(start, LANES)],
            field.at[:, j, pl.ds(SUB + b * SUB, SUB), :],
            sems.at[b, j],
        )

    def begin(b):
        for j in range(own + 2):
            copy(b, j).start()

    def arrive(b):
        for j in range(own + 2):
            copy(b, j).wait()
        at = pl.ds(SUB + b * SUB, SUB)

        @pl.when(first == 0)
        def _():
            for z in range(cells):
                field[z, 0, at, :] = jnp.zeros((SUB, LANES), jnp.int32)

        @pl.when(first + own == tiles)
        def _():
            for z in range(cells):
                field[z, own + 1, at, :] = jnp.zeros((SUB, LANES), jnp.int32)

    return begin, arrive


def stage_kernel(place, own, density_ref, field_ref, sems):
    blocks = density_ref.shape[1] // SUB
    begin, arrive = tile_copies(place, own, density_ref, field_ref, sems)
    for b in range(blocks):
        begin(b)
    lax.fori_loop(0, blocks, lambda b, carry: arrive(b) or carry, 0)


def stage(place, count, density):
    cells, rows, width = density.shape
    own = width // LANES // count
    shape = (cells, own + 2, rows + 2 * SUB, LANES)
    return pl.pallas_call(
        functools.partial(stage_kernel, place, own),
        out_shape=jax.ShapeDtypeStruct(shape, jnp.int32),
        in_specs=[pl.BlockSpec(memory_space=pl.ANY)],
        out_specs=pl.BlockSpec(memory_space=pltpu.VMEM),
        scratch_shapes=[pltpu.SemaphoreType.DMA((rows // SUB, own + 2))],
        compiler_params=pltpu.CompilerParams(vmem_limit_bytes=48 << 20),
        cost_estimate=pl.CostEstimate(
            flops=0, transcendentals=0, bytes_accessed=8 * cells * rows * (own + 2) * LANES
        ),
        name="stage",
    )(density)


def integrate_kernel(
    place, own, staged, flip_ref, coeff_ref, density_ref, zlo_ref, zhi_ref, ylo_ref, yhi_ref,
    token_ref, out_ref, *scratch,
):
    if staged:
        field, (zlo_f, zhi_f, top_f, bottom_f) = token_ref, scratch
    else:
        field, zlo_f, zhi_f, sems = scratch
    _, width = zlo_ref.shape
    cells, rows = ylo_ref.shape[0], zlo_ref.shape[0]
    tiles = width // LANES
    blocks = rows // SUB
    count = tiles // own
    position = lax.axis_index("depth")
    first = first_tile(place, own)
    if not staged:
        begin, arrive = tile_copies(place, own, density_ref, field, sems)
        for b in range(blocks):
            begin(b)
    flip = flip_ref[0]
    for j in range(own):
        cols = pl.ds(pl.multiple_of((first + j) * LANES, LANES), LANES)
        zlo_f[j] = zlo_ref[:, cols].astype(jnp.float32) - CENTRE
        zhi_f[j] = zhi_ref[:, cols].astype(jnp.float32) - CENTRE
        top = ylo_ref[:, cols].astype(jnp.float32).astype(jnp.int32)
        bottom = yhi_ref[:, cols].astype(jnp.float32).astype(jnp.int32)
        if staged:
            top_f[j] = top
            bottom_f[j] = bottom
        for z in range(0 if staged else cells):
            field[z, j + 1, SUB - 1 : SUB, :] = top[z : z + 1]
            field[z, j + 1, SUB + rows : SUB + rows + 1, :] = bottom[z : z + 1]

    coeffs = []
    for row in range(4):
        scale = LOG2E if row == 0 else -LOG2E
        coeffs.append([coeff_ref[row, k] * (scale / CENTRE**k) for k in range(4)])
    sign = jnp.where(flip == 1, 1.0, -1.0)
    rate = sign * OPACITY
    lx, ly = LIGHT[0] / LIGHT[2], LIGHT[1] / LIGHT[2]
    ambient = 0.35 / (0.65 * LIGHT[2])
    lane = lax.broadcasted_iota(jnp.int32, (SUB, LANES), 1)
    first_lane = lane == 0
    last_lane = lane == LANES - 1
    base = (position * cells).astype(jnp.float32)
    step = 1.0 / (cells * count)
    start = (base + 0.5) * step
    finish = (base + (cells - 0.5)) * step
    h_first = jnp.where(flip == 1, 1.0 - start, start)
    h_last = jnp.where(flip == 1, 1.0 - finish, finish)
    delta = jnp.where(flip == 1, -step, step)

    def poly(c, t):
        return c[0] + t * (c[1] + t * (c[2] + t * c[3]))

    row = lax.broadcasted_iota(jnp.int32, (SUB, LANES), 0)
    if not staged:
        arrive(0)

    def block(b, carry):
        if not staged:

            @pl.when(b + 1 < blocks)
            def _():
                arrive(b + 1)

        r = pl.multiple_of(b * SUB, SUB)
        for j in range(1, own + 1):
            column(r, j)
        return carry

    def column(r, j):
        at = pl.ds(r + SUB, SUB)
        zero = jnp.zeros((SUB, LANES), jnp.float32)
        tau = zero
        factor = jnp.ones((SUB, LANES), jnp.float32)
        between = zero
        sums = [zero] * 6
        below = zlo_f[j - 1, pl.ds(r, SUB), :]
        raw = field[0, j, at, :]
        here = raw.astype(jnp.float32) - CENTRE
        for z in range(cells):
            if z + 1 < cells:
                raw_above = field[z + 1, j, at, :]
                above = raw_above.astype(jnp.float32) - CENTRE
            else:
                raw_above = raw
                above = zhi_f[j - 1, pl.ds(r, SUB), :]
            left = pltpu.roll(jnp.where(last_lane, field[z, j - 1, at, :], raw), 1, 1)
            right = pltpu.roll(jnp.where(first_lane, field[z, j + 1, at, :], raw), LANES - 1, 1)
            gx = (right - left).astype(jnp.float32)
            up = field[z, j, pl.ds(r + SUB + 1, SUB), :]
            down = field[z, j, pl.ds(r + SUB - 1, SUB), :]
            if staged:
                up = jnp.where(row + r == rows - 1, bottom_f[j - 1, z : z + 1, :], up)
                down = jnp.where(row + r == 0, top_f[j - 1, z : z + 1, :], down)
            gy = (up - down).astype(jnp.float32)
            gz = above - below
            norm = lax.rsqrt(gx * gx + gy * gy + (gz * gz + 255.0 * 255.0))
            shade = ambient + jnp.abs((lx * gx + ly * gy + gz) * norm)
            tau = tau + jnp.log2(1.0 + jnp.exp2(poly(coeffs[0], here)))
            following = jnp.exp2(rate * tau)
            weight = following - factor
            factor = following
            if z < cells - 1:
                between = between + following
            tilt = weight * norm
            lit = weight * shade
            terms = [lit * (1.0 / (1.0 + jnp.exp2(poly(coeffs[k], here)))) for k in (1, 2, 3)]
            terms += [tilt * gx, tilt * gy, tilt * gz]
            sums = [s + t for s, t in zip(sums, terms)]
            below, here, raw = here, above, raw_above
        inverse = 1.0 / factor
        flipped = flip == 1
        scale = jnp.where(flipped, inverse, -1.0)
        out = pl.ds(r, SUB)
        for k in range(3):
            out_ref[k, j - 1, out, :] = sums[k] * (scale * (0.65 * LIGHT[2]))
            out_ref[k + 5, j - 1, out, :] = sums[k + 3] * scale
        out_ref[3, j - 1, out, :] = 1.0 - jnp.where(flipped, inverse, factor)
        out_ref[4, j - 1, out, :] = (h_last * factor - h_first - delta * between) * scale

    lax.fori_loop(0, blocks, block, 0)


def integrate(place, count, view_flip, tf_coeff, density, zlo, zhi, ylo, yhi, token, staged):
    cells, rows, width = density.shape
    own = width // LANES // count
    smem = pl.BlockSpec(memory_space=pltpu.SMEM)
    vmem = pl.BlockSpec(memory_space=pltpu.VMEM)
    anywhere = pl.BlockSpec(memory_space=pl.ANY)
    voxels = cells * rows * own * LANES
    copied = pltpu.VMEM((cells, own + 2, rows + 2 * SUB, LANES), jnp.int32)
    borders = [pltpu.VMEM((own, rows, LANES), jnp.float32)] * 2
    line = pltpu.VMEM((own, cells, LANES), jnp.int32)
    sems = pltpu.SemaphoreType.DMA((rows // SUB, own + 2))
    return pl.pallas_call(
        functools.partial(integrate_kernel, place, own, staged),
        out_shape=jax.ShapeDtypeStruct((8, own, rows, LANES), jnp.float32),
        in_specs=[smem, smem, anywhere] + [vmem] * 4 + [vmem if staged else anywhere],
        out_specs=vmem,
        scratch_shapes=(borders + [line, line]) if staged else ([copied] + borders + [sems]),
        compiler_params=pltpu.CompilerParams(vmem_limit_bytes=(40 if staged else 52) << 20),
        cost_estimate=pl.CostEstimate(
            flops=70 * voxels, transcendentals=0, bytes_accessed=8 * voxels
        ),
        name="integrate",
    )(view_flip, tf_coeff, view_flip if staged else density, zlo, zhi, ylo, yhi, token)


def shade_kernel(inner, core_ref, halo_ref, *rest):
    if inner:
        out_ref, planes, feats, buf_a, buf_b, acc = rest
    else:
        top_ref, bottom_ref, done_ref, out_ref, planes, feats, buf_a, buf_b, acc = rest
    _, tiles, rows, _ = core_ref.shape
    blocks = rows // SUB
    chosen = list(range(1, blocks - 1)) if inner else [0, blocks - 1]
    needed = sorted({n for b in chosen for n in (b - 1, b, b + 1)})

    def at(n):
        return pl.ds(SUB + n * SUB, SUB)

    for k in range(8):
        for n in needed:
            for t in (0, tiles + 1):
                planes[k, t, at(n), :] = jnp.zeros((SUB, LANES), jnp.float32)
            if 0 <= n < blocks:
                here = slice(n * SUB, n * SUB + SUB)
                side = halo_ref[here, :]
                for j in range(tiles):
                    planes[k, j + 1, at(n), :] = core_ref[k, j, here, :]
            else:
                ref = top_ref if n < 0 else bottom_ref
                side = ref[8 * tiles]
                for j in range(tiles):
                    planes[k, j + 1, at(n), :] = ref[k * tiles + j]
            left = side[:, RADIUS * k : RADIUS * k + RADIUS]
            right = side[:, RADIUS * (8 + k) : RADIUS * (9 + k)]
            planes[k, 0, at(n), LANES - RADIUS : LANES] = left
            planes[k, tiles + 1, at(n), 0:RADIUS] = right

    def features(t, carry):
        for n in needed:
            red, green, blue, alpha, depth, nx, ny, nz = [planes[k, t, at(n), :] for k in range(8)]
            facing = jnp.maximum(LIGHT[0] * nx + LIGHT[1] * ny + LIGHT[2] * nz, 0.0)
            lit = 0.4 + 0.6 * facing
            level = (DEPTH_W * LOG2E) * depth * depth
            level = level + (NORMAL_W * LOG2E) * (nx * nx + ny * ny + nz * nz)
            feats[0, t, at(n), :] = jnp.log2(jnp.maximum(alpha, 1e-37)) - level
            feats[1, t, at(n), :] = depth
            feats[2, t, at(n), :] = nx
            feats[3, t, at(n), :] = ny
            feats[4, t, at(n), :] = nz
            feats[5, t, at(n), :] = red * lit
            feats[6, t, at(n), :] = green * lit
            feats[7, t, at(n), :] = blue * lit
        return carry

    lax.fori_loop(0, tiles + 2, features, 0)
    lane = lax.broadcasted_iota(jnp.int32, (SUB, LANES), 1)

    def shift_setup(index):
        offset = index - RADIUS + (index >= RADIUS).astype(jnp.int32)
        run = offset.astype(jnp.float32)
        spread = -(SPATIAL * LOG2E) * run * run
        border = jnp.where(offset < 0, LANES + offset, offset)
        amount = jnp.where(offset > 0, LANES - offset, -offset)
        below = lane < border
        take_other = (below & (offset >= 0)) | (jnp.logical_not(below) & (offset < 0))
        return jnp.where(offset < 0, 0, 2), amount, take_other, spread

    def moved(setup, k, j, n):
        other, amount, take_other, spread = setup
        mixed = jnp.where(take_other, feats[k, j + other, at(n), :], feats[k, j + 1, at(n), :])
        result = pltpu.roll(mixed, amount, 1)
        return result + spread if k == 0 else result

    for k in range(4):
        for j in range(tiles):
            for b in chosen:
                acc[k, j, at(b), :] = jnp.zeros((SUB, LANES), jnp.float32)

    offsets = sorted({o for b in chosen for o in range(SUB * b - RADIUS, SUB * b + RADIUS + 1)})

    def taps(buf, side, next_index, next_buf):
        pending, items = [], []
        if next_buf is not None:
            setup = shift_setup(next_index)
            items = [(k, j, n) for j in range(tiles) for n in needed for k in range(8)]
        pace = -(-len(items) // (len(offsets) * tiles))

        def pump(last=False):
            for _ in range(pace):
                if items:
                    pending.append((moved(setup, *items[0]),) + items.pop(0))
            while len(pending) > (0 if last else AHEAD):
                value, k, j, n = pending.pop(0)
                next_buf[k, j, at(n), :] = value

        for j in range(tiles):
            own, sums = {}, {}
            for o in offsets:
                pump()
                q = [buf[k, j + side, pl.ds(SUB + o, SUB), :] for k in range(8)]
                for b in chosen:
                    dy = o - SUB * b
                    if abs(dy) > RADIUS:
                        continue
                    if dy == -RADIUS:
                        own[b] = [feats[1, j + 1, at(b), :] * (2.0 * DEPTH_W * LOG2E)]
                        own[b] += [
                            feats[k, j + 1, at(b), :] * (2.0 * NORMAL_W * LOG2E) for k in (2, 3, 4)
                        ]
                        sums[b] = [acc[k, j, at(b), :] for k in range(4)]
                    p, s = own[b], sums[b]
                    power = (q[0] + p[0] * q[1]) + (p[1] * q[2] + p[2] * q[3])
                    power = power + (p[3] * q[4] - SPATIAL * LOG2E * dy * dy)
                    weight = jnp.exp2(power)
                    sums[b] = [s[k] + weight * q[5 + k] for k in range(3)] + [s[3] + weight]
                    if dy == RADIUS:
                        for k in range(4):
                            acc[k, j, at(b), :] = sums[b][k]
        while items or pending:
            pump(not items)

    def pair(step, carry):
        taps(buf_a, 0, 2 * step + 1, buf_b)
        taps(buf_b, 0, jnp.minimum(2 * step + 2, 2 * RADIUS - 1), buf_a)
        return carry

    taps(feats, 1, jnp.int32(0), buf_a)
    lax.fori_loop(0, RADIUS, pair, 0)

    if not inner:
        for k in range(3):
            out_ref[k, SUB : rows - SUB, :] = done_ref[k, SUB : rows - SUB, :]
    for j in range(tiles):
        for b in chosen:
            depth, nx, ny, nz = [feats[k, j + 1, at(b), :] for k in (1, 2, 3, 4)]
            own = (DEPTH_W * LOG2E) * depth * depth
            own = own + (NORMAL_W * LOG2E) * (nx * nx + ny * ny + nz * nz)
            level = jnp.exp2(-own)
            scale = level / (1.0 + level * acc[3, j, at(b), :])
            for k in range(3):
                out_ref[k, b * SUB : b * SUB + SUB, j * LANES : (j + 1) * LANES] = (
                    acc[k, j, at(b), :] * scale
                )


def shade(inner, core, *rest):
    _, tiles, rows, _ = core.shape
    vmem = pl.BlockSpec(memory_space=pltpu.VMEM)
    wide = (8, tiles + 2, rows + 2 * SUB, LANES)
    moved = (8, tiles, rows + 2 * SUB, LANES)
    part = rows - 2 * SUB if inner else 2 * SUB
    work = part * tiles * LANES * (2 * RADIUS + 1) ** 2
    return pl.pallas_call(
        functools.partial(shade_kernel, inner),
        out_shape=jax.ShapeDtypeStruct((3, rows, tiles * LANES), jnp.float32),
        in_specs=[vmem] * (1 + len(rest)),
        out_specs=vmem,
        scratch_shapes=[
            pltpu.VMEM(wide, jnp.float32),
            pltpu.VMEM(wide, jnp.float32),
            pltpu.VMEM(moved, jnp.float32),
            pltpu.VMEM(moved, jnp.float32),
            pltpu.VMEM((4, tiles, rows + 2 * SUB, LANES), jnp.float32),
        ],
        compiler_params=pltpu.CompilerParams(vmem_limit_bytes=24 << 20),
        cost_estimate=pl.CostEstimate(
            flops=16 * work, transcendentals=work, bytes_accessed=8 * rows * tiles * LANES * 4
        ),
        name="shade_inner" if inner else "shade_outer",
    )(core, *rest)


def compose_kernel(base, pieces, mode, leads_ref, *refs):
    images, at_ref = [], 0
    for n in pieces:
        images.append(refs[at_ref : at_ref + n])
        at_ref += n
    outs = refs[at_ref:]
    _, tiles, rows, _ = outs[0].shape
    halves = outs if mode == "halves" else outs[:1]

    def plane(parts, k):
        size = 8 // len(parts)
        return parts[k // size], k % size

    def one(t, carry):
        j = t // (rows // SUB)
        at = pl.ds(pl.multiple_of(t % (rows // SUB) * SUB, SUB), SUB)

        def read(parts):
            found = [plane(parts, k) for k in range(8)]
            return [ref[k, j, at, :] for ref, k in found]

        current = read(images[0])
        for level, parts in enumerate(images[1:]):
            other = read(parts)
            leads = leads_ref[base + level] == 1
            share = jnp.where(leads, 1.0, 1.0 - other[3])
            other_share = jnp.where(leads, 1.0 - current[3], 1.0)
            current = [c * share + o * other_share for c, o in zip(current, other)]
        for k in range(8):
            ref, kk = plane(halves, k)
            ref[kk, j, at, :] = current[k]
        return carry

    lax.fori_loop(0, tiles * (rows // SUB), one, 0)
    if mode == "borders":
        out_ref, last_ref, first_ref = outs
        last_ref[...] = jnp.zeros((rows, LANES), jnp.float32)
        first_ref[...] = jnp.zeros((rows, LANES), jnp.float32)
        for k in range(8):
            last_ref[:, RADIUS * k : RADIUS * k + RADIUS] = out_ref[
                k, tiles - 1, :, LANES - RADIUS : LANES
            ]
            first_ref[:, RADIUS * (8 + k) : RADIUS * (9 + k)] = out_ref[k, 0, :, 0:RADIUS]


def compose(base, mode, leads, *images):
    images = [i if isinstance(i, (tuple, list)) else (i,) for i in images]
    _, tiles, rows, _ = images[0][0].shape
    smem = pl.BlockSpec(memory_space=pltpu.SMEM)
    vmem = pl.BlockSpec(memory_space=pltpu.VMEM)
    whole = jax.ShapeDtypeStruct((8, tiles, rows, LANES), jnp.float32)
    half = jax.ShapeDtypeStruct((4, tiles, rows, LANES), jnp.float32)
    border = jax.ShapeDtypeStruct((rows, LANES), jnp.float32)
    outs = {"plain": (whole,), "halves": (half, half), "borders": (whole, border, border)}[mode]
    parts = [p for image in images for p in image]
    return pl.pallas_call(
        functools.partial(compose_kernel, base, [len(i) for i in images], mode),
        out_shape=outs,
        in_specs=[smem] + [vmem] * len(parts),
        out_specs=[vmem] * len(outs),
        compiler_params=pltpu.CompilerParams(vmem_limit_bytes=8 << 20),
        cost_estimate=pl.CostEstimate(
            flops=0, transcendentals=0, bytes_accessed=32 * tiles * rows * LANES
        ),
        name="compose",
    )(leads, *parts)


def reverse_bits(value, rounds):
    result = 0
    for level in range(rounds):
        result = result * 2 + (value >> level) % 2
    return result


def per_device(density, view_flip, tf_coeff):
    cells, rows, width = density.shape
    count = lax.axis_size("depth")
    position = lax.axis_index("depth")
    flipped = view_flip[0]
    rounds = count.bit_length() - 1
    high = count // 4
    first_plane, last_plane, first_line, last_line = edges(density)
    up, down = shifts("depth")
    zlo = lax.ppermute(last_plane, "depth", up)
    zhi = lax.ppermute(first_plane, "depth", down)
    up, down = shifts("tile")
    ylo = lax.ppermute(last_line, "tile", up)
    yhi = lax.ppermute(first_line, "tile", down)

    def quarter(core_bit, chip_bit, token):
        parts = []
        for h in range(high):
            place = (core_bit, chip_bit, h)
            given = stage(place, count, density) if token is None else token
            parts.append(
                integrate(
                    place, count, view_flip, tf_coeff, density, zlo, zhi, ylo, yhi, given,
                    token is None,
                )
            )
        return parts[0] if high == 1 else jnp.concatenate(parts, axis=1)

    bits = [position // 2**level % 2 for level in range(rounds)]
    leads = jnp.stack([bit == flipped for bit in bits]).astype(jnp.int32)
    far_given = quarter(1, 1, None)
    far_partner = swapped(far_given, "depth", 0)
    far_kept = quarter(0, 1, far_given)
    far = compose(0, "halves", leads, far_kept, far_partner)
    chip_partner = [swapped(far[0], "depth", 1)]
    near_given = quarter(1, 0, far[0])
    near_partner = swapped(near_given, "depth", 0)
    token, behind = lax.optimization_barrier((chip_partner[0], far[1]))
    chip_partner.append(swapped(behind, "depth", 1))
    near_kept = quarter(0, 0, token)
    images, base = [near_kept, near_partner, chip_partner], 0
    own = width // LANES // count
    if high > 1:
        current = compose(0, "plain", leads, *images)[0]
        order = [reverse_bits(place, rounds - 2) for place in range(high)]
        current = jnp.concatenate([current[:, p * own : (p + 1) * own] for p in order], axis=1)
        for level in range(2, rounds):
            half = current.shape[1] // 2
            kept = lax.dynamic_slice_in_dim(current, bits[level] * half, half, 1)
            given = lax.dynamic_slice_in_dim(current, (1 - bits[level]) * half, half, 1)
            partner = swapped(given, "depth", level)
            images, base = [kept, partner], level
            if level < rounds - 1:
                current = compose(level, "plain", leads, kept, partner)[0]
    core, last, first = compose(base, "borders", leads, *images)
    up, down = shifts("depth")
    halo = lax.ppermute(last, "depth", up) + lax.ppermute(first, "depth", down)
    inner = shade(True, core, halo)
    up, down = shifts("tile")

    def band(start):
        rows_at = slice(start, start + SUB)
        image = core[:, :, rows_at].reshape(8 * own, SUB, LANES)
        return jnp.concatenate([image, halo[None, rows_at]], axis=0)

    top = lax.ppermute(band(rows - SUB), "tile", up)
    bottom = lax.ppermute(band(0), "tile", down)
    return shade(False, core, halo, top, bottom, inner)


def solution(mesh):
    in_specs = (P("depth", "tile", None), P("tile"), P())
    out_specs = P(None, "tile", "depth")
    return jax.shard_map(
        per_device, mesh=mesh, in_specs=in_specs, out_specs=out_specs, check_vma=False
    )
```
